128 devices in a mesh: tm: 4 (over y), space: 32 (over x, z, core).
Axes of the slice: x: 4, y: 4, z: 4, core: 2. Of those that a mesh axis runs over, the one named last changes fastest.
Arguments:
- vectors: bfloat16 [8, 2, 3, 16384, 384], P('tm', None, None, 'space'), may hold values from -6 to 6
- perambulators: bfloat16 [128, 2, 384, 384], P(('tm', 'space')), may hold values from -0.0007324219 to 0.0007324219
- item_block: int32 [128, 128], P(('tm', 'space')), may hold values from 0 to 3
- item_owner: int32 [128, 128], P(('tm', 'space')), may hold values from 0 to 127, as said below
- momenta: int32 [2, 3], replicated, may hold values from -2 to 2, as said below
Outputs:
- contracted: bfloat16 [128, 128, 2, 12, 768], P(('tm', 'space'))
The draws below stay inside these ranges and needn't reach their ends.
Inputs may be any that keep to these rules, and one draw needn't show every extreme that they name: `item_owner`: in every device's list no owner appears more than 2 times, and some owners appear exactly 2 times in the lists of all devices. `momenta`: the first component of every momentum is nonzero.
All inputs are finite; a program needn't handle non-finite values.
Results may differ from the reference program's by a relative error of at most 0.0057.
Values may be sent and summed in bfloat16 or wider, within the bound.
A program may use at most 128 MiB of HBM per device.

```python
import math
import jax
import jax.numpy as jnp
from jax import lax

N_EV = 384
LX = 64
NMOM = 2
CAP = 2
TS_DEV = 2
RB = 12
BLK = 4
T_SLAB = 8
SITES = 16384
ITEMS = 128
N_TM = 4
N_SPACE = 32
DEVICES = 128


def draw_item_owner(key, part):
    shuffle_key = jax.random.fold_in(key, 101)
    noise_key = jax.random.fold_in(key, 102)
    order_key = jax.random.fold_in(key, 103)
    heavy_count = max(1, DEVICES // 16)
    owner_order = jax.random.permutation(shuffle_key, DEVICES)
    owner_rank = jnp.zeros((DEVICES,), jnp.int32).at[owner_order].set(jnp.arange(DEVICES, dtype=jnp.int32))
    position_list = jnp.arange(DEVICES * CAP, dtype=jnp.int32)
    position_owner = position_list // CAP
    heavy_slot = owner_rank[position_owner] < heavy_count
    noise_draw = jax.random.randint(noise_key, (DEVICES, DEVICES * CAP), 0, 1 << 20)
    scores = jnp.where(heavy_slot[None, :], (1 << 29) + position_list[None, :], noise_draw * (DEVICES * CAP) + position_list[None, :])
    top_scores, picked = lax.top_k(scores, ITEMS)
    mixing = jax.random.randint(order_key, (DEVICES, ITEMS), 0, 1 << 20) * ITEMS + jnp.arange(ITEMS, dtype=jnp.int32)[None, :]
    arrangement = jnp.argsort(mixing, axis=1)
    picked = jnp.take_along_axis(picked, arrangement, axis=1)
    return position_owner[picked].astype(jnp.int32)


def draw_momenta(key, part):
    magnitude = jax.random.randint(jax.random.fold_in(key, 201), (NMOM,), 1, 3)
    direction_sign = jax.random.randint(jax.random.fold_in(key, 202), (NMOM,), 0, 2) * 2 - 1
    remaining = jax.random.randint(jax.random.fold_in(key, 203), (NMOM, 2), -2, 3)
    return jnp.concatenate([(magnitude * direction_sign)[:, None], remaining], axis=1).astype(jnp.int32)


def set_ends(array, rng, low, largest):
    longest = array.shape.index(max(array.shape))
    spots = []
    for shift in (0, 1):
        where = [jax.random.randint(jax.random.fold_in(rng, axis), (), 0, length) for axis, length in enumerate(array.shape)]
        where[longest] = (where[longest] + shift) % array.shape[longest]
        spots.append(tuple(where))
    return array.at[spots[0]].set(low).at[spots[1]].set(largest)


def block_levels(stream_key, extent, cuts, smallest, top_value):
    def one(dim, parts):
        steps = jax.random.uniform(jax.random.fold_in(jax.random.fold_in(stream_key, 6), dim), (parts,), jnp.float32, smallest / len(cuts), top_value / len(cuts))
        return jnp.repeat(jnp.exp(steps), extent[dim] // parts).reshape((-1,) + (1,) * (len(extent) - dim - 1))

    loudness = one(*cuts[0])
    for cut in cuts[1:]:
        loudness = loudness * one(*cut)
    return loudness


def scatter_about(rng, shape, deviation, reach, pieces=(), held_as=jnp.bfloat16):
    drawn = jax.random.normal(rng, shape, jnp.float32) * deviation
    if len(pieces) > 0:
        drawn = block_levels(rng, shape, pieces, -0.22, 0.18) * drawn
    return jnp.clip(drawn, min=-reach, max=reach).astype(held_as)


def setup_inputs(seed: int = 0) -> dict:
    key_of = jax.random.split(jax.random.key(seed), 6)
    return {
        "vectors": scatter_about(key_of[0], (T_SLAB, 2, 3, SITES, N_EV), 1.0, 6.0, ((0, 4), (3, 32))),
        "perambulators": scatter_about(key_of[1], (DEVICES, 2, N_EV, N_EV), (12 * N_EV * SITES) ** -0.5, 0.0007324219, ((0, 128),)),
        "item_block": set_ends(jax.random.randint(key_of[2], (DEVICES, ITEMS), 0, BLK), jax.random.fold_in(key_of[2], 1), 0, BLK - 1).astype(jnp.int32),
        "item_owner": draw_item_owner(jax.random.fold_in(key_of[5], 71), 0),
        "momenta": draw_momenta(jax.random.fold_in(key_of[5], 71), 0),
    }


def site_phase(momenta, first_site, site_count):
    site_index = first_site + jnp.arange(site_count, dtype=jnp.int32)
    coord_x = site_index % LX
    coord_y = (site_index // LX) % LX
    coord_z = site_index // (LX * LX)
    phase_turns = (momenta[:, 0:1] * coord_x[None, :] + momenta[:, 1:2] * coord_y[None, :] + momenta[:, 2:3] * coord_z[None, :]) % LX
    phase_angle = phase_turns.astype(jnp.float32) * (2.0 * math.pi / LX)
    return jnp.cos(phase_angle), jnp.sin(phase_angle)


def twisted_right(vectors, cosines, sines):
    real_part = vectors[:, 0].astype(jnp.float32)[:, None]
    imag_part = vectors[:, 1].astype(jnp.float32)[:, None]
    cosine = cosines[None, :, None, :, None]
    sine_term = sines[None, :, None, :, None]
    twisted_real = (cosine * real_part + sine_term * imag_part).astype(jnp.bfloat16)
    twisted_imag = (cosine * imag_part - sine_term * real_part).astype(jnp.bfloat16)
    upper_half = jnp.stack([twisted_real, twisted_imag], axis=2)
    lower_half = jnp.stack([twisted_imag, -twisted_real], axis=2)
    shape_lead = upper_half.shape
    inner_rows = shape_lead[2] * shape_lead[3] * shape_lead[4]
    return jnp.concatenate([upper_half.reshape(shape_lead[0], shape_lead[1], inner_rows, shape_lead[5]), lower_half.reshape(shape_lead[0], shape_lead[1], inner_rows, shape_lead[5])], axis=-1)


def slot_table(block_ids, owners, devices, pad_block):
    item_count = owners.shape[0]
    position_list = jnp.arange(item_count, dtype=jnp.int32)
    earlier = (owners[None, :] == owners[:, None]) & (position_list[None, :] < position_list[:, None])
    slot_rank = jnp.sum(earlier.astype(jnp.int32), axis=1)
    target = owners * CAP + slot_rank
    return jnp.full((devices * CAP,), pad_block, jnp.int32).at[target].set(block_ids.astype(jnp.int32))


def complex_kernel(pair):
    top_rows = jnp.concatenate([pair[0], pair[1]], axis=1)
    bottom_rows = jnp.concatenate([-pair[1], pair[0]], axis=1)
    return jnp.concatenate([top_rows, bottom_rows], axis=0)


def reference(vectors, perambulators, item_block, item_owner, momenta):
    cosines, sines = site_phase(momenta, 0, SITES)
    elementals = []
    for slab_index in range(T_SLAB):
        right_side = twisted_right(vectors[slab_index:slab_index + 1], cosines, sines)[0]
        left_side = vectors[slab_index].reshape(-1, N_EV)
        per_mom = [jnp.dot(left_side.T, right_side[mom_index], preferred_element_type=jnp.float32) for mom_index in range(NMOM)]
        elementals.append(jnp.stack(per_mom))
    elemental = jnp.stack(elementals).astype(jnp.bfloat16)
    blocks = elemental.reshape(N_TM, TS_DEV, NMOM, N_SPACE, RB, 2 * N_EV).transpose(0, 3, 1, 2, 4, 5).reshape(DEVICES, BLK, RB, 2 * N_EV)
    blocks = jnp.concatenate([blocks, jnp.zeros((DEVICES, 1, RB, 2 * N_EV), jnp.bfloat16)], axis=1)
    tables = jax.vmap(lambda block_ids, owners: slot_table(block_ids, owners, DEVICES, BLK))(item_block, item_owner)
    senders = jnp.arange(DEVICES, dtype=jnp.int32)

    def per_owner(owner_index):
        block_slots = lax.dynamic_slice_in_dim(tables, (owner_index * CAP).astype(jnp.int32), CAP, 1)
        chosen = blocks[senders[:, None], block_slots]
        kernel = complex_kernel(lax.dynamic_index_in_dim(perambulators, owner_index, 0, keepdims=False))
        product = jnp.dot(chosen.reshape(-1, 2 * N_EV), kernel, preferred_element_type=jnp.float32)
        return product.astype(jnp.bfloat16).reshape(DEVICES, CAP, RB, 2 * N_EV)

    return lax.map(per_owner, senders)
```

```python
import math

import jax
import jax.numpy as jnp
from jax import lax
from jax.sharding import Mesh
from jax.sharding import PartitionSpec as P

LX = 64
CAP = 2
SPACE = ("space_0", "space_1", "space_2")
TM_SPACE = ("tm", "space_0", "space_1", "space_2")


def site_phase(momenta, first_site, site_count):
    site_index = first_site + jnp.arange(site_count, dtype=jnp.int32)
    coord_x = site_index % LX
    coord_y = site_index // LX % LX
    coord_z = site_index // (LX * LX)
    phase_turns = (
        momenta[:, 0:1] * coord_x[None, :]
        + momenta[:, 1:2] * coord_y[None, :]
        + momenta[:, 2:3] * coord_z[None, :]
    ) % LX
    phase_angle = phase_turns.astype(jnp.float32) * (2.0 * math.pi / LX)
    return (jnp.cos(phase_angle), jnp.sin(phase_angle))


def twisted_right(vectors, cosines, sines):
    real_part = vectors[:, 0].astype(jnp.float32)[:, None]
    imag_part = vectors[:, 1].astype(jnp.float32)[:, None]
    cosine = cosines[None, :, None, :, None]
    sine_term = sines[None, :, None, :, None]
    twisted_real = (cosine * real_part + sine_term * imag_part).astype(jnp.bfloat16)
    twisted_imag = (cosine * imag_part - sine_term * real_part).astype(jnp.bfloat16)
    upper_half = jnp.stack([twisted_real, twisted_imag], axis=2)
    lower_half = jnp.stack([twisted_imag, -twisted_real], axis=2)
    shape_lead = upper_half.shape
    inner_rows = shape_lead[2] * shape_lead[3] * shape_lead[4]
    return jnp.concatenate(
        [
            upper_half.reshape(shape_lead[0], shape_lead[1], inner_rows, shape_lead[5]),
            lower_half.reshape(shape_lead[0], shape_lead[1], inner_rows, shape_lead[5]),
        ],
        axis=-1,
    )


def slot_ids(lists, me, pad_block):
    mine = lists[:, 1, :] == me
    item_count = lists.shape[2]
    upper = jnp.triu(jnp.ones((item_count, item_count), jnp.bfloat16))
    rank = jnp.dot(mine.astype(jnp.bfloat16), upper, preferred_element_type=jnp.float32)
    shifted = lists[:, 0, :] - pad_block
    picks = [
        jnp.sum(jnp.where(mine & (rank == float(s + 1)), shifted, 0), axis=1) for s in range(CAP)
    ]
    return jnp.stack(picks, axis=1) + pad_block


def complex_kernel(pair):
    top_rows = jnp.concatenate([pair[0], pair[1]], axis=1)
    bottom_rows = jnp.concatenate([-pair[1], pair[0]], axis=1)
    return jnp.concatenate([top_rows, bottom_rows], axis=0)


def body(vectors, perambulators, item_block, item_owner, momenta):
    group_count = lax.axis_size("tm")
    space_count = lax.axis_size(SPACE)
    devices = group_count * space_count
    slab_count = vectors.shape[0]
    site_count = vectors.shape[3]
    vector_width = vectors.shape[4]
    first_site = lax.axis_index(SPACE) * site_count
    cosines, sines = site_phase(momenta, first_site, site_count)
    right_side = twisted_right(vectors, cosines, sines)
    left_side = vectors.reshape(slab_count, -1, vector_width)
    partial_value = jnp.einsum(
        "tmk,tpmj->tpkj", left_side, right_side, preferred_element_type=jnp.float32
    )
    row_block = vector_width // space_count
    full_width = partial_value.shape[3]
    block_total = slab_count * momenta.shape[0]
    flat = partial_value.astype(jnp.bfloat16).reshape(-1, full_width)
    blocks = lax.psum_scatter(flat, SPACE, scatter_dimension=0, tiled=True)
    lists = lax.all_gather(jnp.concatenate([item_block, item_owner], axis=0), TM_SPACE)
    ids = slot_ids(lists, lax.axis_index(TM_SPACE), block_total)
    everyone = lax.all_gather(blocks, TM_SPACE, tiled=True).reshape(-1, row_block, full_width)
    padded = jnp.concatenate([everyone, jnp.zeros((1, row_block, full_width), jnp.bfloat16)], axis=0)
    device = jnp.arange(devices)[:, None]
    place = (device // space_count * block_total + ids) * space_count + device % space_count
    rows = jnp.where(ids < block_total, place, devices * block_total)
    received = jnp.take(padded, rows.reshape(-1), axis=0)
    kernel = complex_kernel(perambulators[0])
    product = jnp.dot(received.reshape(-1, full_width), kernel, preferred_element_type=jnp.float32)
    result = product.astype(jnp.bfloat16).reshape(devices, CAP, row_block, full_width)
    return result[None]


def solution(mesh):
    split = Mesh(
        mesh.devices.reshape(mesh.shape["tm"], 4, 4, 2), ("tm", "space_0", "space_1", "space_2")
    )
    in_specs = (
        P("tm", None, None, SPACE, None),
        P(TM_SPACE, None, None, None),
        P(TM_SPACE, None),
        P(TM_SPACE, None),
        P(),
    )
    out_specs = P(TM_SPACE, None, None, None, None)
    return jax.shard_map(body, mesh=split, in_specs=in_specs, out_specs=out_specs, check_vma=False)
```

```python
import functools
import math

import jax
import jax.numpy as jnp
from jax import lax
from jax.experimental import pallas as pl
from jax.experimental.pallas import tpu as pltpu
from jax.sharding import PartitionSpec as P

LX = 64
CAP = 2
RING = 4
CHIPS = RING * RING * RING
PLANE = RING * RING
LANES = 128
BF = jnp.bfloat16
F32 = jnp.float32
MESH = pl.DeviceIdType.MESH

Y, X, Z = 0, 1, 2
CUBE = ((X, 0), (Y, 0), (Z, 0), (X, 1), (Y, 1), (Z, 1))
FACE = ((X, 0), (Z, 0), (X, 1), (Z, 1))


def gray_bit(position, bit):
    return position // 2 if bit else (position % 2 + position // 2) % 2


def across(position, bit):
    return 3 - position if bit else position + 1 - 2 * (position % 2)


def cube_dim(order, stage):
    return CUBE[(order + stage) % 6]


def face_dim(order, stage):
    return FACE[(order + stage) % 4]


def cube_index(place, order):
    return sum(gray_bit(place[a], b) * (1 << s) for s, (a, b) in enumerate(cube_dim(order, s) for s in range(6)))


def face_index(place, order):
    return sum(gray_bit(place[a], b) * (8 >> s) for s, (a, b) in enumerate(face_dim(order, s) for s in range(4)))


def gather_kernel(
    mom,
    vec,
    blk_in,
    own_in,
    picked,
    v,
    vt,
    tab,
    acc,
    full,
    outbox,
    inbox,
    mine,
    every,
    lists,
    ids,
    rows,
    local_sem,
    v_sem,
    list_sem,
    rs_sem,
    ag_sem,
    sib_sem,
    row_sem,
):
    sites, width = v.shape[3], v.shape[4]
    half = width
    rb = width // PLANE
    y = lax.axis_index("tm")
    sp = lax.axis_index("space")
    x, z, k = sp // 8, (sp // 2) % 4, sp % 2
    place = (y, x, z)

    def device(where, core):
        return (where[0], where[1] * 8 + where[2] * 2 + core)

    def neighbour(dim):
        axis, bit = dim
        where = list(place)
        where[axis] = across(place[axis], bit)
        return device(where, k)

    sibling = device(place, 1 - k)

    def remote(src, dst, sems, to):
        return pltpu.make_async_remote_copy(
            src_ref=src, dst_ref=dst, send_sem=sems.at[0], recv_sem=sems.at[1], device_id=to, device_id_type=MESH
        )

    barrier = pltpu.get_barrier_semaphore()
    for dim in CUBE:
        pl.semaphore_signal(barrier, inc=1, device_id=neighbour(dim), device_id_type=MESH)
    pl.semaphore_signal(barrier, inc=1, device_id=sibling, device_id_type=MESH)
    load_v = pltpu.make_async_copy(vec.at[k], v.at[0], local_sem.at[0])
    load_v.start()
    my_cube = [cube_index(place, j) for j in range(6)]
    list_pair = my_cube[0]
    load_blk = pltpu.make_async_copy(blk_in, lists.at[list_pair, k, pl.ds(0, 1)], local_sem.at[1])
    load_own = pltpu.make_async_copy(own_in, lists.at[list_pair, k, pl.ds(1, 1)], local_sem.at[2])
    load_blk.start()
    load_own.start()
    pl.semaphore_wait(barrier, len(CUBE) + 1)

    send_v = remote(vec.at[1 - k], v.at[1], v_sem, sibling)
    send_v.start()
    load_blk.wait()
    load_own.wait()

    def list_copy(stage):
        if stage == 0:
            ref = lists.at[list_pair, k]
            return remote(ref, ref, list_sem.at[:, 0], sibling)
        size = 1 << (stage - 1)
        ref = lists.at[pl.ds(list_pair // size * size, size)]
        return remote(ref, ref, list_sem.at[:, stage], neighbour(cube_dim(0, stage - 1)))

    def list_step(stage):
        if stage > 0:
            list_copy(stage - 1).wait()
        if stage < 7:
            list_copy(stage).start()

    list_step(0)

    lane = lax.broadcasted_iota(jnp.int32, (8, 2 * sites), 1)
    row = lax.broadcasted_iota(jnp.int32, (8, 2 * sites), 0)
    side = lane // sites
    site = (2 * (sp // 2) + jnp.where(side == 0, k, 1 - k)) * sites + lane % sites
    gx, gy, gz = site % LX, site // LX % LX, site // (LX * LX)

    def turns(p):
        return mom[p, 0] * gx + mom[p, 1] * gy + mom[p, 2] * gz

    turn = jnp.where(row < 2, turns(0), turns(1)) - (LX // 4) * (row % 2)
    tab[...] = jnp.transpose(jnp.cos((turn & (LX - 1)).astype(F32) * (2.0 * math.pi / LX)))

    def rs_range(q, stage):
        size = 8 >> stage
        me = face_index(place, q)
        base = me // (2 * size) * (2 * size)
        bit = me // size % 2
        return size, base + bit * size, base + (1 - bit) * size

    def rs_copy(q, stage):
        size, _, other = rs_range(q, stage)
        return remote(
            outbox.at[q, pl.ds(other, size)],
            inbox.at[q, pl.ds(16 - 2 * size, size)],
            rs_sem.at[:, q, stage],
            neighbour(face_dim(q, stage)),
        )

    def rs_finish(q, stage):
        rs_copy(q, stage).wait_recv()
        size, keep, _ = rs_range(q, stage)
        p, h = q // 2, q % 2
        if stage < 3:

            def add(i, carry):
                total = full[q, keep + i] + inbox[q, 16 - 2 * size + i].astype(F32)
                full[q, keep + i] = total
                outbox[q, keep + i] = total.astype(BF)
                return carry

            lax.fori_loop(0, size, add, 0)
            rs_copy(q, stage + 1).start()
        else:
            total = (full[q, keep] + inbox[q, 14].astype(F32)).astype(BF)
            for jj in range(3):
                mine[h * 3 + jj, p] = total[:, jj * LANES : (jj + 1) * LANES]

    for step in range(4):
        s, p = step // 2, step % 2
        if step == 0:
            load_v.wait()
        if step == 2:
            send_v.wait_recv()

        def color(c, carry, s=s, p=p):
            vr, vi = v[s, 0, c], v[s, 1, c]
            if p == 0:
                vt[c, :, :sites] = jnp.transpose(vr)
                vt[c, :, sites:] = jnp.transpose(vi)
            cos = tab[s * sites : (s + 1) * sites, 2 * p : 2 * p + 1]
            sin = tab[s * sites : (s + 1) * sites, 2 * p + 1 : 2 * p + 2]
            fr, fi = vr.astype(F32), vi.astype(F32)
            tr = (cos * fr + sin * fi).astype(BF)
            ti = (cos * fi - sin * fr).astype(BF)
            real = jnp.concatenate([tr, ti], axis=0)
            imag = jnp.concatenate([ti, -tr], axis=0)
            part = jnp.dot(vt[c], jnp.concatenate([real, imag], axis=1), preferred_element_type=F32)
            if s == 0:

                @pl.when(c == 0)
                def _():
                    acc[p] = part

                @pl.when(c != 0)
                def _():
                    acc[p] = acc[p] + part
            else:
                acc[p] = acc[p] + part
            return carry

        lax.fori_loop(0, 3, color, 0)
        list_step(step + 1)
        if s == 1:
            for h in range(2):
                q = p * 2 + h
                for chip in range(PLANE):
                    i = face_index((0, chip // 4, chip % 4), q)
                    tile = acc[p, chip * rb : (chip + 1) * rb, h * half : (h + 1) * half]
                    full[q, i] = tile
                    outbox[q, i] = tile.astype(BF)
                rs_copy(q, 0).start()

    for stage in range(4):
        for q in range(4):
            rs_finish(q, stage)
        if stage < 3:
            list_step(stage + 5)

    def held(j, level):
        size = 1 << level
        return every.at[k, j, pl.ds(my_cube[j] // size * size, size)]

    def other_half(j, level):
        size = 1 << level
        start = my_cube[j] // size
        start = start + 1 - 2 * (start % 2)
        return every.at[k, j, pl.ds(start * size, size)]

    def ag_copy(j, stage, late):
        piece = held if not late else other_half
        ref = piece(j, max(stage - 1, 0))
        return remote(ref, ref, ag_sem.at[:, j, stage, late], neighbour(cube_dim(j, stage)))

    def ag_wait(j, stage):
        size = 1 << stage
        arrived = other_half(j, stage)
        if stage == 0:
            remote(arrived, arrived, ag_sem.at[:, j, 0, 0], sibling).wait_recv()
            return
        for part in range(2):
            piece = every.at[k, j, pl.ds(0, size // 2)]
            remote(piece, piece, ag_sem.at[:, j, stage, part], sibling).wait_recv()

    def sib_copy(j, n):
        ref = held(j, 0) if n == 0 else other_half(j, n - 1)
        return remote(ref, ref, sib_sem.at[:, j, n], sibling)

    for j in range(6):
        every[k, j, my_cube[j]] = mine[j]
        ag_copy(j, 0, 0).start()
        ag_copy(j, 1, 0).start()
        sib_copy(j, 0).start()
    for stage in range(6):
        for j in range(6):
            ag_wait(j, stage)
            if stage < 5:
                ag_copy(j, stage + 1, 1).start()
            if stage < 4:
                ag_copy(j, stage + 2, 0).start()
            sib_copy(j, stage + 1).start()
        if stage == 1:
            me = y * 32 + sp
            at = lax.broadcasted_iota(jnp.int32, (CHIPS, LANES), 1)
            cols = []
            for core in range(2):
                block = lists[:, core, 0, :]
                hit = lists[:, core, 1, :] == me
                first = jnp.min(jnp.where(hit, at, LANES), axis=1, keepdims=True)
                last = jnp.max(jnp.where(hit, at, -1), axis=1, keepdims=True)
                cols.append(jnp.sum(jnp.where(at == first, block + 1, 0), axis=1, keepdims=True) - 1)
                cols.append(
                    jnp.sum(jnp.where((at == last) & (last > first), block + 1, 0), axis=1, keepdims=True) - 1
                )
            table = jnp.full((CHIPS, LANES), -1, jnp.int32)
            for n, col in enumerate(cols):
                table = jnp.where(at == n, col, table)
            ids[...] = table
    for j in range(6):
        for n in range(7):
            sib_copy(j, n).wait_recv()

    out_rows = 2 * CAP * (rb // 2)
    in_rows = 4 * rb
    rho = lax.broadcasted_iota(jnp.int32, (out_rows, in_rows), 0)
    kappa = lax.broadcasted_iota(jnp.int32, (out_rows, in_rows), 1)
    slot, r, core = rho % 2, rho % rb // 2, rho // rb
    target = core * (rb // 2) + r

    def pick(c, carry):
        where = (c // 16, c // 4 % 4, c % 4)
        order = [cube_index(where, j) for j in range(6)]
        bands = []
        for u in range(2):
            for p in range(2):
                bands.append(jnp.concatenate([every[u, j, order[j], p] for j in range(6)], axis=1))
        source = jnp.concatenate(bands, axis=0)
        listed = ids[pl.ds(order[0], 1), :]
        one = jnp.where(slot == 0, listed[:, 0:1], listed[:, 1:2])
        two = jnp.where(slot == 0, listed[:, 2:3], listed[:, 3:4])
        want = jnp.where(core == 0, one, two) * rb + target
        chosen = (kappa == want).astype(F32).astype(BF)
        rows[pl.ds(pl.multiple_of(c * out_rows, out_rows), out_rows), :] = jnp.dot(
            chosen, source, preferred_element_type=F32
        ).astype(BF)
        return carry

    lax.fori_loop(0, CHIPS, pick, 0)
    store = pltpu.make_async_copy(rows, picked, row_sem)
    store.start()

    send_v.wait_send()
    for stage in range(4):
        for q in range(4):
            rs_copy(q, stage).wait_send()
    for j in range(6):
        for stage in range(6):
            for late in range(2 if stage else 1):
                ag_copy(j, stage, late).wait_send()
        for n in range(7):
            sib_copy(j, n).wait_send()
    store.wait()


def product_kernel(rows, pair, out, kernel):
    width = pair.shape[1]

    @pl.when(pl.program_id(0) == 0)
    def _():
        kernel[:width, :width] = pair[0]
        kernel[:width, width:] = pair[1]
        kernel[width:, :width] = -pair[1]
        kernel[width:, width:] = pair[0]

    y = jnp.dot(rows[...], kernel[...], preferred_element_type=F32).astype(BF)
    out[...] = y.reshape(out.shape)


def body(vectors, perambulators, item_block, item_owner, momenta):
    sites, width = vectors.shape[3], vectors.shape[4]
    devices = 2 * CHIPS
    rb = width // PLANE
    total = devices * CAP * (rb // 2)
    anywhere = pl.BlockSpec(memory_space=pl.ANY)
    picked = pl.pallas_call(
        gather_kernel,
        out_shape=jax.ShapeDtypeStruct((total, 2 * width), BF),
        in_specs=[pl.BlockSpec(memory_space=pltpu.SMEM), anywhere, anywhere, anywhere],
        out_specs=anywhere,
        scratch_shapes=[
            pltpu.VMEM((2, 2, 3, sites, width), BF),
            pltpu.VMEM((3, width, 2 * sites), BF),
            pltpu.VMEM((2 * sites, 8), F32),
            pltpu.VMEM((2, width, 2 * width), F32),
            pltpu.VMEM((4, PLANE, rb, width), F32),
            pltpu.VMEM((4, PLANE, rb, width), BF),
            pltpu.VMEM((4, PLANE, rb, width), BF),
            pltpu.VMEM((6, 2, rb, LANES), BF),
            pltpu.VMEM((2, 6, CHIPS, 2, rb, LANES), BF),
            pltpu.VMEM((CHIPS, 2, 2, LANES), jnp.int32),
            pltpu.VMEM((CHIPS, LANES), jnp.int32),
            pltpu.VMEM((total, 2 * width), BF),
            pltpu.SemaphoreType.DMA((3,)),
            pltpu.SemaphoreType.DMA((2,)),
            pltpu.SemaphoreType.DMA((2, 7)),
            pltpu.SemaphoreType.DMA((2, 4, 4)),
            pltpu.SemaphoreType.DMA((2, 6, 6, 2)),
            pltpu.SemaphoreType.DMA((2, 6, 7)),
            pltpu.SemaphoreType.DMA,
        ],
        compiler_params=pltpu.CompilerParams(
            collective_id=0, has_side_effects=True, vmem_limit_bytes=56 * 1024 * 1024
        ),
        name="gather_elementals",
    )(momenta, vectors, item_block, item_owner)
    tile = 384
    out = pl.pallas_call(
        product_kernel,
        out_shape=jax.ShapeDtypeStruct((total // 2, 2, 2 * width), BF),
        grid=(total // tile,),
        in_specs=[
            pl.BlockSpec((tile, 2 * width), lambda i: (i, 0)),
            pl.BlockSpec((2, width, width), lambda i: (0, 0, 0)),
        ],
        out_specs=pl.BlockSpec((tile // 2, 2, 2 * width), lambda i: (i, 0, 0)),
        scratch_shapes=[pltpu.VMEM((2 * width, 2 * width), BF)],
        compiler_params=pltpu.CompilerParams(vmem_limit_bytes=32 * 1024 * 1024),
        name="contract_perambulators",
    )(picked, perambulators[0])
    return out.reshape(1, devices, rb // 2, CAP, 2 * width).transpose(0, 1, 3, 2, 4)


def solution(mesh):
    both = ("tm", "space")
    in_specs = (
        P("tm", None, None, "space", None),
        P(both, None, None, None),
        P(both, None),
        P(both, None),
        P(),
    )
    out_specs = P(both, None, None, None, None)
    return jax.shard_map(body, mesh=mesh, in_specs=in_specs, out_specs=out_specs, check_vma=False)
```

```python
import math

import jax
import jax.numpy as jnp
from jax import lax
from jax.experimental import pallas as pl
from jax.experimental.pallas import tpu as pltpu
from jax.sharding import PartitionSpec as P

LX = 64
CAP = 2
RING = 4
CHIPS = RING * RING * RING
PLANE = RING * RING
LANES = 128
BF = jnp.bfloat16
F32 = jnp.float32
MESH = pl.DeviceIdType.MESH

Y, X, Z = 0, 1, 2
REDUCE_AXES = ((X, Z), (Z, X), (X, Z), (Z, X), (X, Z), (Z, X))
GATHER_AXES = ((Y, X, Z), (X, Z, Y), (Z, Y, X), (Y, Z, X), (X, Y, Z), (Z, X, Y))
LIST_AXES = (X, Z, Y)


def plane_index(place, j):
    a, b = REDUCE_AXES[j]
    return place[a] * 4 + place[b]


def chip_index(place, axes):
    a, b, c = axes
    return place[c] * 16 + place[b] * 4 + place[a]


def gather_kernel(
    mom,
    vec,
    blk_in,
    own_in,
    picked,
    v,
    vt,
    vn,
    tw,
    tab,
    core_out,
    core_in,
    full,
    outbox,
    inbox,
    inbox2,
    every,
    lists,
    ids,
    rows,
    local_sem,
    core_sem,
    list_sem,
    rs_sem,
    ag_sem,
    last_sem,
    fwd_sem,
    sib_sem,
    row_sem,
):
    sites, width = v.shape[3], v.shape[4]
    colors = v.shape[2]
    rb = 2 * width // PLANE
    y = lax.axis_index("tm")
    sp = lax.axis_index("space")
    x, z, k = sp // 8, (sp // 2) % 4, sp % 2
    place = (y, x, z)

    def device(where, core):
        return (where[0], where[1] * 8 + where[2] * 2 + core)

    def ring(axis, offset):
        where = list(place)
        where[axis] = (place[axis] + offset) % RING
        return where[axis], device(where, k)

    sibling = device(place, 1 - k)

    def remote(src, dst, sems, to):
        return pltpu.make_async_remote_copy(
            src_ref=src, dst_ref=dst, send_sem=sems.at[0], recv_sem=sems.at[1], device_id=to, device_id_type=MESH
        )

    barrier = pltpu.get_barrier_semaphore()
    for axis in (Y, X, Z):
        for offset in (1, 2, 3):
            pl.semaphore_signal(barrier, inc=1, device_id=ring(axis, offset)[1], device_id_type=MESH)
    pl.semaphore_signal(barrier, inc=1, device_id=sibling, device_id_type=MESH)

    def load(n, c):
        slab = (1 - k) if n == 0 else k
        return pltpu.make_async_copy(vec.at[slab, :, c], v.at[n, :, c], local_sem.at[n * colors + c])

    for n in range(2):
        for c in range(colors):
            load(n, c).start()
    my_list = chip_index(place, LIST_AXES)
    load_blk = pltpu.make_async_copy(blk_in, lists.at[my_list, k, pl.ds(0, 1)], local_sem.at[2 * colors])
    load_own = pltpu.make_async_copy(own_in, lists.at[my_list, k, pl.ds(1, 1)], local_sem.at[2 * colors + 1])
    load_blk.start()
    load_own.start()

    def list_copies(stage):
        if stage == 0:
            ref = lists.at[my_list, k]
            return [remote(ref, ref, list_sem.at[:, 0, 0], sibling)]
        size = 4 ** (stage - 1)
        ref = lists.at[pl.ds(my_list // size * size, size)]
        axis = LIST_AXES[stage - 1]
        return [remote(ref, ref, list_sem.at[:, stage, o - 1], ring(axis, o)[1]) for o in (1, 2, 3)]

    def list_step(stage):
        if stage > 0:
            for copy in list_copies(stage - 1):
                copy.wait()
        if stage < 4:
            for copy in list_copies(stage):
                copy.start()

    lane = lax.broadcasted_iota(jnp.int32, (8, sites), 1)
    row = lax.broadcasted_iota(jnp.int32, (8, sites), 0)
    site = sp * sites + lane
    gx, gy, gz = site % LX, site // LX % LX, site // (LX * LX)

    def turns(p):
        return mom[p, 0] * gx + mom[p, 1] * gy + mom[p, 2] * gz

    turn = jnp.where(row < 2, turns(0), turns(1)) - (LX // 4) * (row % 2)
    tab[...] = jnp.transpose(jnp.cos((turn & (LX - 1)).astype(F32) * (2.0 * math.pi / LX)))

    def twist(n):
        def color(c, carry):
            vr, vi = v[n, 0, c], v[n, 1, c]
            tr, ti = jnp.transpose(vr), jnp.transpose(vi)
            vt[c, :, :sites] = tr
            vt[c, :, sites:] = ti
            vn[c, :, :sites] = -ti
            vn[c, :, sites:] = tr
            fr, fi = vr.astype(F32), vi.astype(F32)
            for p in range(2):
                cos = tab[:, 2 * p : 2 * p + 1]
                sin = tab[:, 2 * p + 1 : 2 * p + 2]
                tw[c, :sites, p * width : (p + 1) * width] = (cos * fr + sin * fi).astype(BF)
                tw[c, sites:, p * width : (p + 1) * width] = (cos * fi - sin * fr).astype(BF)
            return carry

        for c in range(colors):
            load(n, c).wait()
        lax.fori_loop(0, colors, color, 0)

    def product(h):
        left = vn if h else vt
        total = jnp.dot(left[0], tw[0], preferred_element_type=F32)
        for c in range(1, colors):
            total = total + jnp.dot(left[c], tw[c], preferred_element_type=F32)
        return total

    def piece(total, chip):
        p, i = chip // (PLANE // 2), chip % (PLANE // 2)
        return total[i * rb : (i + 1) * rb, p * width : (p + 1) * width]

    def core_copy(h):
        return remote(core_out.at[h], core_in.at[h], core_sem.at[:, h], sibling)

    def rs1_copies(j):
        copies = []
        for o in (1, 2, 3):
            at, to = ring(REDUCE_AXES[j][0], o)
            copies.append(
                remote(outbox.at[j, pl.ds(at * 4, 4)], inbox.at[j, o - 1], rs_sem.at[:, j, 0, o - 1], to)
            )
        return copies

    def rs2_copies(j):
        copies = []
        for o in (1, 2, 3):
            at, to = ring(REDUCE_AXES[j][1], o)
            row_of = place[REDUCE_AXES[j][0]] * 4 + at
            copies.append(remote(outbox.at[j, row_of], inbox2.at[j, o - 1], rs_sem.at[:, j, 1, o - 1], to))
        return copies

    def rs1_start(j):
        for copy in rs1_copies(j):
            copy.start()

    def rs1_finish(j):
        for copy in rs1_copies(j):
            copy.wait_recv()
        base = place[REDUCE_AXES[j][0]] * 4
        for b in range(4):
            total = full[j, base + b]
            for o in range(3):
                total = total + inbox[j, o, b].astype(F32)
            full[j, base + b] = total
            outbox[j, base + b] = total.astype(BF)
        for copy in rs2_copies(j):
            copy.start()

    def rs2_finish(j):
        for copy in rs2_copies(j):
            copy.wait_recv()
        total = full[j, plane_index(place, j)]
        for o in range(3):
            total = total + inbox2[j, o].astype(F32)
        every[k, j, my_chip[j]] = total.astype(BF)

    my_chip = [chip_index(place, axes) for axes in GATHER_AXES]

    def block(j, start, size):
        return every.at[k, j, pl.ds(start, size)]

    def group(j, c, b):
        return block(j, c * 16 + b * 4, 4)

    def coords(j):
        a, b, c = GATHER_AXES[j]
        return place[a], place[b], place[c]

    def ag1_copies(j):
        ref = block(j, my_chip[j], 1)
        return [remote(ref, ref, ag_sem.at[:, j, 0, o - 1], ring(GATHER_AXES[j][0], o)[1]) for o in (1, 2, 3)]

    def ag2_copies(j):
        _, b, c = coords(j)
        ref = group(j, c, b)
        return [remote(ref, ref, ag_sem.at[:, j, 1, o - 1], ring(GATHER_AXES[j][1], o)[1]) for o in (1, 2, 3)]

    def ag3_copy(j, g, way):
        _, b, c = coords(j)
        ref = group(j, c, (b + g) % RING)
        return remote(ref, ref, last_sem.at[:, j, g, way], ring(GATHER_AXES[j][2], 1 if way == 0 else 3)[1])

    def fwd_copy(j, g):
        _, b, c = coords(j)
        way = g // 2
        source = (c + (3 if way == 0 else 1)) % RING
        ref = group(j, source, (b + g) % RING)
        return remote(ref, ref, fwd_sem.at[:, j, g], ring(GATHER_AXES[j][2], 1 if way == 0 else 3)[1])

    def sib_copy(j, n):
        _, b, c = coords(j)
        if n < 4:
            ref = group(j, c, (b + n) % RING)
        elif n < 6:
            ref = block(j, (c + (3 if n == 4 else 1)) % RING * 16, 16)
        else:
            ref = block(j, (c + 2) % RING * 16, 16)
        return remote(ref, ref, sib_sem.at[:, j, n], sibling)

    def ag1_start(j):
        for copy in ag1_copies(j):
            copy.start()

    def ag1_finish(j):
        for copy in ag1_copies(j):
            copy.wait_recv()
        for copy in ag2_copies(j):
            copy.start()
        for way in range(2):
            ag3_copy(j, 0, way).start()
        sib_copy(j, 0).start()

    def ag2_finish(j):
        for o, copy in zip((1, 2, 3), ag2_copies(j)):
            copy.wait_recv()
            g = 4 - o
            for way in range(2):
                ag3_copy(j, g, way).start()
            sib_copy(j, g).start()

    def ag3_finish(j):
        for g in range(4):
            ag3_copy(j, g, g // 2).wait_recv()
            fwd_copy(j, g).start()
        for g in range(4):
            ag3_copy(j, g, 1 - g // 2).wait_recv()
        sib_copy(j, 4).start()
        sib_copy(j, 5).start()

    def ag4_finish(j):
        for g in range(4):
            fwd_copy(j, g).wait_recv()
        sib_copy(j, 6).start()

    twist(0)
    for h in range(2):
        total = product(h)
        for chip in range(PLANE):
            core_out[h, chip] = piece(total, chip).astype(BF)
        if h == 0:
            pl.semaphore_wait(barrier, 10)
            load_blk.wait()
            load_own.wait()
        core_copy(h).start()
        list_step(h)
    twist(1)
    for h in range(2):
        total = product(h)
        core_copy(h).wait_recv()
        for chip in range(PLANE):
            both = piece(total, chip) + core_in[h, chip].astype(F32)
            for jj in range(3):
                j = h * 3 + jj
                i = plane_index((0, chip // 4, chip % 4), j)
                tile = both[:, jj * LANES : (jj + 1) * LANES]
                full[j, i] = tile
                outbox[j, i] = tile.astype(BF)
        for jj in range(3):
            rs1_start(h * 3 + jj)
        list_step(h + 2)
    for j in range(6):
        rs1_finish(j)
    for j in range(6):
        rs2_finish(j)
        ag1_start(j)
    list_step(4)

    me = y * 32 + sp
    at = lax.broadcasted_iota(jnp.int32, (CHIPS, LANES), 1)
    table = jnp.full((CHIPS, LANES), -1, jnp.int32)
    for core in range(2):
        listed = lists[:, core, 0, :] + 1
        hit = lists[:, core, 1, :] == me
        first = jnp.min(jnp.where(hit, at, LANES), axis=1, keepdims=True)
        last = jnp.max(jnp.where(hit, at, -1), axis=1, keepdims=True)
        one = jnp.sum(jnp.where(at == first, listed, 0), axis=1, keepdims=True) - 1
        two = jnp.sum(jnp.where((at == last) & (last > first), listed, 0), axis=1, keepdims=True) - 1
        table = jnp.where(at == 2 * core, one, jnp.where(at == 2 * core + 1, two, table))
    ids[...] = table

    for j in range(6):
        ag1_finish(j)
    for j in range(6):
        ag2_finish(j)
    for j in range(6):
        ag3_finish(j)
    for j in range(6):
        ag4_finish(j)
    for j in range(6):
        for n in range(7):
            sib_copy(j, n).wait_recv()

    own_rows = rb // 4
    out_rows = 4 * CAP * own_rows
    in_rows = 4 * rb
    rho = lax.broadcasted_iota(jnp.int32, (out_rows, in_rows), 0)
    kappa = lax.broadcasted_iota(jnp.int32, (out_rows, in_rows), 1)
    dev = rho // (CAP * own_rows)
    target = dev * own_rows + rho // CAP % own_rows
    which = dev * CAP + rho % CAP

    def pick(n, carry):
        gy_, g = n // 8, n % 8
        bands = []
        for u in range(2):
            for p in range(2):
                where = (gy_, p * 2 + g // 4, g % 4)
                bands.append(
                    jnp.concatenate([every[u, j, chip_index(where, GATHER_AXES[j])] for j in range(6)], axis=1)
                )
        source = jnp.concatenate(bands, axis=0)
        want = target
        for half in range(2):
            chip = chip_index((gy_, g // 2, g % 2 * 2 + half), LIST_AXES)
            listed = ids[pl.ds(chip, 1), :]
            for lane_ in range(4):
                want = jnp.where(which == half * 4 + lane_, target + listed[:, lane_ : lane_ + 1] * rb, want)
        chosen = (kappa == want).astype(F32).astype(BF)
        rows[pl.ds(pl.multiple_of(n * out_rows, out_rows), out_rows), :] = jnp.dot(
            chosen, source, preferred_element_type=F32
        ).astype(BF)
        return carry

    lax.fori_loop(0, CHIPS // 2, pick, 0)
    store = pltpu.make_async_copy(rows, picked, row_sem)
    store.start()

    for h in range(2):
        core_copy(h).wait_send()
    for j in range(6):
        for copy in rs1_copies(j) + rs2_copies(j) + ag1_copies(j) + ag2_copies(j):
            copy.wait_send()
        for g in range(4):
            for way in range(2):
                ag3_copy(j, g, way).wait_send()
            fwd_copy(j, g).wait_send()
        for g in range(4):
            pass
        for n in range(7):
            sib_copy(j, n).wait_send()
    store.wait()


def product_kernel(rows, pair, out, kernel):
    width = pair.shape[1]

    @pl.when(pl.program_id(0) == 0)
    def _():
        kernel[:width, :width] = pair[0]
        kernel[:width, width:] = pair[1]
        kernel[width:, :width] = -pair[1]
        kernel[width:, width:] = pair[0]

    y = jnp.dot(rows[...], kernel[...], preferred_element_type=F32).astype(BF)
    out[...] = y.reshape(out.shape)


def body(vectors, perambulators, item_block, item_owner, momenta):
    colors, sites, width = vectors.shape[2:]
    devices = 2 * CHIPS
    rb = 2 * width // PLANE
    own_rows = rb // 4
    total = devices * CAP * own_rows
    anywhere = pl.BlockSpec(memory_space=pl.ANY)
    picked = pl.pallas_call(
        gather_kernel,
        out_shape=jax.ShapeDtypeStruct((total, 2 * width), BF),
        in_specs=[pl.BlockSpec(memory_space=pltpu.SMEM), anywhere, anywhere, anywhere],
        out_specs=anywhere,
        scratch_shapes=[
            pltpu.VMEM((2, 2, colors, sites, width), BF),
            pltpu.VMEM((colors, width, 2 * sites), BF),
            pltpu.VMEM((colors, width, 2 * sites), BF),
            pltpu.VMEM((colors, 2 * sites, 2 * width), BF),
            pltpu.VMEM((sites, 8), F32),
            pltpu.VMEM((2, PLANE, rb, width), BF),
            pltpu.VMEM((2, PLANE, rb, width), BF),
            pltpu.VMEM((6, PLANE, rb, LANES), F32),
            pltpu.VMEM((6, PLANE, rb, LANES), BF),
            pltpu.VMEM((6, 3, 4, rb, LANES), BF),
            pltpu.VMEM((6, 3, rb, LANES), BF),
            pltpu.VMEM((2, 6, CHIPS, rb, LANES), BF),
            pltpu.VMEM((CHIPS, 2, 2, LANES), jnp.int32),
            pltpu.VMEM((CHIPS, LANES), jnp.int32),
            pltpu.VMEM((total, 2 * width), BF),
            pltpu.SemaphoreType.DMA((2 * colors + 2,)),
            pltpu.SemaphoreType.DMA((2, 2)),
            pltpu.SemaphoreType.DMA((2, 4, 3)),
            pltpu.SemaphoreType.DMA((2, 6, 2, 3)),
            pltpu.SemaphoreType.DMA((2, 6, 2, 3)),
            pltpu.SemaphoreType.DMA((2, 6, 4, 2)),
            pltpu.SemaphoreType.DMA((2, 6, 4)),
            pltpu.SemaphoreType.DMA((2, 6, 7)),
            pltpu.SemaphoreType.DMA,
        ],
        compiler_params=pltpu.CompilerParams(
            collective_id=0, has_side_effects=True, vmem_limit_bytes=56 * 1024 * 1024
        ),
        name="gather_elementals",
    )(momenta, vectors, item_block, item_owner)
    tile = 384
    out = pl.pallas_call(
        product_kernel,
        out_shape=jax.ShapeDtypeStruct((total // 2, 2, 2 * width), BF),
        grid=(total // tile,),
        in_specs=[
            pl.BlockSpec((tile, 2 * width), lambda i: (i, 0)),
            pl.BlockSpec((2, width, width), lambda i: (0, 0, 0)),
        ],
        out_specs=pl.BlockSpec((tile // 2, 2, 2 * width), lambda i: (i, 0, 0)),
        scratch_shapes=[pltpu.VMEM((2 * width, 2 * width), BF)],
        compiler_params=pltpu.CompilerParams(vmem_limit_bytes=56 * 1024 * 1024),
        name="contract_perambulators",
    )(picked, perambulators[0])
    return out.reshape(1, devices, own_rows, CAP, 2 * width).transpose(0, 1, 3, 2, 4)


def solution(mesh):
    both = ("tm", "space")
    in_specs = (
        P("tm", None, None, "space", None),
        P(both, None, None, None),
        P(both, None),
        P(both, None),
        P(),
    )
    out_specs = P(both, None, None, None, None)
    return jax.shard_map(body, mesh=mesh, in_specs=in_specs, out_specs=out_specs, check_vma=False)
```

```python
import math

import jax
import jax.numpy as jnp
from jax import lax
from jax.experimental import pallas as pl
from jax.experimental.pallas import tpu as pltpu
from jax.sharding import PartitionSpec as P

LX = 64
CAP = 2
RING = 4
CHIPS = RING * RING * RING
PLANE = RING * RING
LANES = 128
BF = jnp.bfloat16
F32 = jnp.float32
MESH = pl.DeviceIdType.MESH

Y, X, Z = 0, 1, 2
REDUCE_AXES = ((X, Z), (Z, X), (X, Z), (Z, X), (X, Z), (Z, X))
GATHER_AXES = ((X, Z, Y), (Y, Z, X), (X, Z, Y), (X, Y, Z), (X, Z, Y), (Z, Y, X))
LIST_AXES = (Z, X, Y)
STAGE_AT = (0.0, 2.2, 5.6, 8.7, 12.2, 15.7, 20.7, 24.2)
CHOOSE_AT = 21.3


def plane_index(place, j):
    a, b = REDUCE_AXES[j]
    return place[a] * 4 + place[b]


def chip_index(place, axes):
    a, b, c = axes
    return place[c] * 16 + place[b] * 4 + place[a]


def gather_kernel(
    mom,
    vec,
    blk_in,
    own_in,
    picked,
    v,
    vt,
    vn,
    tw,
    tab,
    core_out,
    core_in,
    full,
    outbox,
    inbox,
    inbox2,
    every,
    lists,
    ids,
    chosen,
    rows,
    local_sem,
    core_sem,
    list_sem,
    rs_sem,
    ag_sem,
    last_sem,
    fwd_sem,
    sib_sem,
    row_sem,
):
    sites, width = v.shape[3], v.shape[4]
    colors = v.shape[2]
    rb = 2 * width // PLANE
    y = lax.axis_index("tm")
    sp = lax.axis_index("space")
    x, z, k = sp // 8, (sp // 2) % 4, sp % 2
    place = (y, x, z)

    def device(where, core):
        return (where[0], where[1] * 8 + where[2] * 2 + core)

    def ring(axis, offset):
        where = list(place)
        where[axis] = (place[axis] + offset) % RING
        return where[axis], device(where, k)

    sibling = device(place, 1 - k)

    def remote(src, dst, sems, to):
        return pltpu.make_async_remote_copy(
            src_ref=src, dst_ref=dst, send_sem=sems.at[0], recv_sem=sems.at[1], device_id=to, device_id_type=MESH
        )

    barrier = pltpu.get_barrier_semaphore()
    for axis in (Y, X, Z):
        for offset in (1, 2, 3):
            pl.semaphore_signal(barrier, inc=1, device_id=ring(axis, offset)[1], device_id_type=MESH)
    pl.semaphore_signal(barrier, inc=1, device_id=sibling, device_id_type=MESH)

    def load(n, c):
        slab = (1 - k) if n == 0 else k
        return pltpu.make_async_copy(vec.at[slab, :, c], v.at[n, :, c], local_sem.at[n * colors + c])

    for n in range(2):
        for c in range(colors):
            load(n, c).start()
    my_list = chip_index(place, LIST_AXES)
    load_blk = pltpu.make_async_copy(blk_in, lists.at[my_list, k, pl.ds(0, 1)], local_sem.at[2 * colors])
    load_own = pltpu.make_async_copy(own_in, lists.at[my_list, k, pl.ds(1, 1)], local_sem.at[2 * colors + 1])
    load_blk.start()
    load_own.start()

    def list_copies(stage):
        if stage == 0:
            ref = lists.at[my_list, k]
            return [remote(ref, ref, list_sem.at[:, 0, 0], sibling)]
        size = 4 ** (stage - 1)
        ref = lists.at[pl.ds(my_list // size * size, size)]
        axis = LIST_AXES[stage - 1]
        return [remote(ref, ref, list_sem.at[:, stage, o - 1], ring(axis, o)[1]) for o in (1, 2, 3)]

    def list_step(stage):
        if stage > 0:
            for copy in list_copies(stage - 1):
                copy.wait()
        if stage < 4:
            for copy in list_copies(stage):
                copy.start()

    lane = lax.broadcasted_iota(jnp.int32, (8, sites), 1)
    row = lax.broadcasted_iota(jnp.int32, (8, sites), 0)
    site = sp * sites + lane
    gx, gy, gz = site % LX, site // LX % LX, site // (LX * LX)

    def turns(p):
        return mom[p, 0] * gx + mom[p, 1] * gy + mom[p, 2] * gz

    turn = jnp.where(row < 2, turns(0), turns(1)) - (LX // 4) * (row % 2)
    tab[...] = jnp.transpose(jnp.cos((turn & (LX - 1)).astype(F32) * (2.0 * math.pi / LX)))

    def twist(n):
        for c in range(colors):
            load(n, c).wait()
            low, mid, high = 2 * c * sites, (2 * c + 1) * sites, (2 * c + 2) * sites
            vr, vi = v[n, 0, c], v[n, 1, c]
            tr, ti = jnp.transpose(vr), jnp.transpose(vi)
            vt[n, :, low:mid] = tr
            vt[n, :, mid:high] = ti
            vn[n, :, low:mid] = -ti
            vn[n, :, mid:high] = tr
            fr, fi = vr.astype(F32), vi.astype(F32)
            for p in range(2):
                cos = tab[:, 2 * p : 2 * p + 1]
                sin = tab[:, 2 * p + 1 : 2 * p + 2]
                real = (cos * fr + sin * fi).astype(BF)
                imag = (cos * fi - sin * fr).astype(BF)
                for jj in range(3):
                    cols = slice(jj * LANES, (jj + 1) * LANES)
                    tw[n, jj, low:mid, p * LANES : (p + 1) * LANES] = real[:, cols]
                    tw[n, jj, mid:high, p * LANES : (p + 1) * LANES] = imag[:, cols]

    def product(n, j):
        left = vn if j // 3 else vt
        return jnp.dot(left[n], tw[n, j % 3], preferred_element_type=F32)

    def pieces(j):
        for chip in range(PLANE):
            p, i = chip // (PLANE // 2), chip % (PLANE // 2)
            at = plane_index((0, chip // 4, chip % 4), j)
            yield at, slice(i * rb, (i + 1) * rb), slice(p * LANES, (p + 1) * LANES)

    def core_copy(h):
        return remote(core_out.at[h], core_in.at[h], core_sem.at[:, h], sibling)

    def rs1_copies(j):
        copies = []
        for o in (1, 2, 3):
            at, to = ring(REDUCE_AXES[j][0], o)
            copies.append(
                remote(outbox.at[j, pl.ds(at * 4, 4)], inbox.at[j, o - 1], rs_sem.at[:, j, 0, o - 1], to)
            )
        return copies

    def rs2_copies(j):
        copies = []
        for o in (1, 2, 3):
            at, to = ring(REDUCE_AXES[j][1], o)
            row_of = place[REDUCE_AXES[j][0]] * 4 + at
            copies.append(remote(outbox.at[j, row_of], inbox2.at[j, o - 1], rs_sem.at[:, j, 1, o - 1], to))
        return copies

    def rs1_start(j):
        for copy in rs1_copies(j):
            copy.start()

    def rs1_finish(j):
        for copy in rs1_copies(j):
            copy.wait_recv()
        base = place[REDUCE_AXES[j][0]] * 4
        for b in range(4):
            total = full[j, base + b]
            for o in range(3):
                total = total + inbox[j, o, b].astype(F32)
            full[j, base + b] = total
            outbox[j, base + b] = total.astype(BF)
        for copy in rs2_copies(j):
            copy.start()

    def rs2_finish(j):
        for copy in rs2_copies(j):
            copy.wait_recv()
        total = full[j, plane_index(place, j)]
        for o in range(3):
            total = total + inbox2[j, o].astype(F32)
        every[k, j, my_chip[j]] = total.astype(BF)

    my_chip = [chip_index(place, axes) for axes in GATHER_AXES]

    def block(j, start, size):
        return every.at[k, j, pl.ds(start, size)]

    def group(j, c, b):
        return block(j, c * 16 + b * 4, 4)

    def coords(j):
        a, b, c = GATHER_AXES[j]
        return place[a], place[b], place[c]

    def ag1_copies(j):
        ref = block(j, my_chip[j], 1)
        return [remote(ref, ref, ag_sem.at[:, j, 0, o - 1], ring(GATHER_AXES[j][0], o)[1]) for o in (1, 2, 3)]

    def ag2_copies(j):
        _, b, c = coords(j)
        ref = group(j, c, b)
        return [remote(ref, ref, ag_sem.at[:, j, 1, o - 1], ring(GATHER_AXES[j][1], o)[1]) for o in (1, 2, 3)]

    def ag3_copy(j, g, way):
        _, b, c = coords(j)
        ref = group(j, c, (b + g) % RING)
        return remote(ref, ref, last_sem.at[:, j, g, way], ring(GATHER_AXES[j][2], 1 if way == 0 else 3)[1])

    def fwd_copy(j, g):
        _, b, c = coords(j)
        way = g // 2
        source = (c + (3 if way == 0 else 1)) % RING
        ref = group(j, source, (b + g) % RING)
        return remote(ref, ref, fwd_sem.at[:, j, g], ring(GATHER_AXES[j][2], 1 if way == 0 else 3)[1])

    def sib_copy(j, n):
        _, b, c = coords(j)
        if n < 4:
            ref = group(j, c, (b + n) % RING)
        elif n < 6:
            ref = block(j, (c + (3 if n == 4 else 1)) % RING * 16, 16)
        else:
            ref = block(j, (c + 2) % RING * 16, 16)
        return remote(ref, ref, sib_sem.at[:, j, n], sibling)

    def ag1_start(j):
        for copy in ag1_copies(j):
            copy.start()

    def ag1_finish(j):
        for copy in ag1_copies(j):
            copy.wait_recv()
        for copy in ag2_copies(j):
            copy.start()
        for way in range(2):
            ag3_copy(j, 0, way).start()
        sib_copy(j, 0).start()

    def ag2_finish(j):
        for o, copy in zip((1, 2, 3), ag2_copies(j)):
            copy.wait_recv()
            g = 4 - o
            for way in range(2):
                ag3_copy(j, g, way).start()
            sib_copy(j, g).start()

    def ag3_finish(j):
        for g in range(4):
            ag3_copy(j, g, g // 2).wait_recv()
            fwd_copy(j, g).start()
        for g in range(4):
            ag3_copy(j, g, 1 - g // 2).wait_recv()
        sib_copy(j, 4).start()
        sib_copy(j, 5).start()

    def ag4_finish(j):
        for g in range(4):
            fwd_copy(j, g).wait_recv()
        sib_copy(j, 6).start()

    def make_table():
        me = y * 32 + sp
        at = lax.broadcasted_iota(jnp.int32, (CHIPS, LANES), 1)
        table = jnp.full((CHIPS, LANES), -1, jnp.int32)
        for core in range(2):
            listed = lists[:, core, 0, :] + 1
            hit = lists[:, core, 1, :] == me
            first = jnp.min(jnp.where(hit, at, LANES), axis=1, keepdims=True)
            last = jnp.max(jnp.where(hit, at, -1), axis=1, keepdims=True)
            one = jnp.sum(jnp.where(at == first, listed, 0), axis=1, keepdims=True) - 1
            two = jnp.sum(jnp.where((at == last) & (last > first), listed, 0), axis=1, keepdims=True) - 1
            table = jnp.where(at == 2 * core, one, jnp.where(at == 2 * core + 1, two, table))
        ids[...] = table


    own_rows = rb // 4
    out_rows = 4 * CAP * own_rows
    in_rows = 4 * rb
    rho = lax.broadcasted_iota(jnp.int32, (out_rows, CHIPS // 2), 0)
    kappa = lax.broadcasted_iota(jnp.int32, (out_rows, in_rows), 1).astype(F32)
    target = rho // (CAP * own_rows) * own_rows + rho // CAP % own_rows

    def choose_all():
        make_table()
        lane_ = lax.broadcasted_iota(jnp.int32, (out_rows, LANES), 1)
        row_ = lax.broadcasted_iota(jnp.int32, (out_rows, LANES), 0)
        which = row_ // (CAP * own_rows) * CAP + row_ % CAP
        want = target.astype(F32)
        for half in range(2):
            spread = jnp.where(which == half * 4 + lane_, jnp.where(lane_ < 4, rb, 0), 0).astype(F32).astype(BF)
            some = ids[pl.ds(half, CHIPS // 2, stride=2), :].astype(F32).astype(BF)
            want = want + lax.dot_general(spread, some, (((1,), (1,)), ((), ())), preferred_element_type=F32)
        for n in range(CHIPS // 2):
            chosen[n] = (kappa == want[:, n : n + 1]).astype(F32).astype(BF)

    def dots(j):
        total = product(0, j)
        for at, r, c in pieces(j):
            core_out[j, at] = total[r, c].astype(BF)
        total = product(1, j)
        for at, r, c in pieces(j):
            full[j, at] = total[r, c]
        if j == 0:
            pl.semaphore_wait(barrier, 10)
        core_copy(j).start()

    def core_finish(j):
        core_copy(j).wait_recv()
        total = full[j] + core_in[j].astype(F32)
        full[j] = total
        outbox[j] = total.astype(BF)
        rs1_start(j)

    def reduce_finish(j):
        rs2_finish(j)
        ag1_start(j)

    def first_list():
        load_blk.wait()
        load_own.wait()
        list_step(0)

    twist(0)
    twist(1)

    events = [(1.5, first_list, ())]
    events += [(t, list_step, (n + 1,)) for n, t in enumerate((3.7, 7.7, 11.6, 16.6))]
    events += [(CHOOSE_AT, choose_all, ())]
    for j in range(6):
        steps = (dots, core_finish, rs1_finish, reduce_finish, ag1_finish, ag2_finish, ag3_finish, ag4_finish)
        events += [(j + t, step, (j,)) for step, t in zip(steps, STAGE_AT)]
    for _, step, args in sorted(events, key=lambda e: e[0]):
        step(*args)
    for j in range(6):
        for n in range(7):
            sib_copy(j, n).wait_recv()

    def pick(n):
        gy_, g = n // 8, n % 8
        bands = []
        for u in range(2):
            for p in range(2):
                where = (gy_, p * 2 + g // 4, g % 4)
                bands.append(
                    jnp.concatenate([every[u, j, chip_index(where, GATHER_AXES[j])] for j in range(6)], axis=1)
                )
        return jnp.dot(chosen[n], jnp.concatenate(bands, axis=0), preferred_element_type=F32).astype(BF)

    chunk = 4 * out_rows

    def store(i):
        at = pl.ds(pl.multiple_of(i * chunk, chunk), chunk)
        return pltpu.make_async_copy(rows.at[at], picked.at[at], row_sem.at[i])

    def pick_four(i, carry):
        for n in range(4):
            at = pl.ds(pl.multiple_of((i * 4 + n) * out_rows, out_rows), out_rows)
            rows[at, :] = pick(i * 4 + n)
        store(i).start()
        return carry

    lax.fori_loop(0, 8, pick_four, 0)

    for j in range(6):
        core_copy(j).wait_send()
        for copy in rs1_copies(j) + rs2_copies(j) + ag1_copies(j) + ag2_copies(j):
            copy.wait_send()
        for g in range(4):
            for way in range(2):
                ag3_copy(j, g, way).wait_send()
            fwd_copy(j, g).wait_send()
        for n in range(7):
            sib_copy(j, n).wait_send()
    for i in range(8):
        store(i).wait()


def product_kernel(rows, pair, out, kernel):
    width = pair.shape[1]

    @pl.when(pl.program_id(0) == 0)
    def _():
        kernel[:width, :width] = pair[0]
        kernel[:width, width:] = pair[1]
        kernel[width:, :width] = -pair[1]
        kernel[width:, width:] = pair[0]

    y = jnp.dot(rows[...], kernel[...], preferred_element_type=F32).astype(BF)
    out[...] = y.reshape(out.shape)


def body(vectors, perambulators, item_block, item_owner, momenta):
    colors, sites, width = vectors.shape[2:]
    devices = 2 * CHIPS
    rb = 2 * width // PLANE
    own_rows = rb // 4
    total = devices * CAP * own_rows
    anywhere = pl.BlockSpec(memory_space=pl.ANY)
    picked = pl.pallas_call(
        gather_kernel,
        out_shape=jax.ShapeDtypeStruct((total, 2 * width), BF),
        in_specs=[pl.BlockSpec(memory_space=pltpu.SMEM), anywhere, anywhere, anywhere],
        out_specs=anywhere,
        scratch_shapes=[
            pltpu.VMEM((2, 2, colors, sites, width), BF),
            pltpu.VMEM((2, width, 2 * colors * sites), BF),
            pltpu.VMEM((2, width, 2 * colors * sites), BF),
            pltpu.VMEM((2, 3, 2 * colors * sites, 2 * LANES), BF),
            pltpu.VMEM((sites, 8), F32),
            pltpu.VMEM((6, PLANE, rb, LANES), BF),
            pltpu.VMEM((6, PLANE, rb, LANES), BF),
            pltpu.VMEM((6, PLANE, rb, LANES), F32),
            pltpu.VMEM((6, PLANE, rb, LANES), BF),
            pltpu.VMEM((6, 3, 4, rb, LANES), BF),
            pltpu.VMEM((6, 3, rb, LANES), BF),
            pltpu.VMEM((2, 6, CHIPS, rb, LANES), BF),
            pltpu.VMEM((CHIPS, 2, 2, LANES), jnp.int32),
            pltpu.VMEM((CHIPS, LANES), jnp.int32),
            pltpu.VMEM((CHIPS // 2, 8 * own_rows, 4 * rb), BF),
            pltpu.VMEM((total, 2 * width), BF),
            pltpu.SemaphoreType.DMA((2 * colors + 2,)),
            pltpu.SemaphoreType.DMA((2, 6)),
            pltpu.SemaphoreType.DMA((2, 4, 3)),
            pltpu.SemaphoreType.DMA((2, 6, 2, 3)),
            pltpu.SemaphoreType.DMA((2, 6, 2, 3)),
            pltpu.SemaphoreType.DMA((2, 6, 4, 2)),
            pltpu.SemaphoreType.DMA((2, 6, 4)),
            pltpu.SemaphoreType.DMA((2, 6, 7)),
            pltpu.SemaphoreType.DMA((8,)),
        ],
        compiler_params=pltpu.CompilerParams(
            collective_id=0, has_side_effects=True, vmem_limit_bytes=60 * 1024 * 1024
        ),
        name="gather_elementals",
    )(momenta, vectors, item_block, item_owner)
    tile = 384
    out = pl.pallas_call(
        product_kernel,
        out_shape=jax.ShapeDtypeStruct((total // 2, 2, 2 * width), BF),
        grid=(total // tile,),
        in_specs=[
            pl.BlockSpec((tile, 2 * width), lambda i: (i, 0)),
            pl.BlockSpec((2, width, width), lambda i: (0, 0, 0)),
        ],
        out_specs=pl.BlockSpec((tile // 2, 2, 2 * width), lambda i: (i, 0, 0)),
        scratch_shapes=[pltpu.VMEM((2 * width, 2 * width), BF)],
        compiler_params=pltpu.CompilerParams(vmem_limit_bytes=56 * 1024 * 1024),
        name="contract_perambulators",
    )(picked, perambulators[0])
    return out.reshape(1, devices, own_rows, CAP, 2 * width).transpose(0, 1, 3, 2, 4)


def solution(mesh):
    both = ("tm", "space")
    in_specs = (
        P("tm", None, None, "space", None),
        P(both, None, None, None),
        P(both, None),
        P(both, None),
        P(),
    )
    out_specs = P(both, None, None, None, None)
    return jax.shard_map(body, mesh=mesh, in_specs=in_specs, out_specs=out_specs, check_vma=False)
```

```python
import math

import jax
import jax.numpy as jnp
from jax import lax
from jax.experimental import pallas as pl
from jax.experimental.pallas import tpu as pltpu
from jax.sharding import PartitionSpec as P

LX = 64
CAP = 2
RING = 4
CHIPS = RING * RING * RING
PLANE = RING * RING
LANES = 128
BF = jnp.bfloat16
F32 = jnp.float32
MESH = pl.DeviceIdType.MESH

Y, X, Z = 0, 1, 2
REDUCE_AXES = ((X, Z), (Z, X), (X, Z), (Z, X), (X, Z), (Z, X))
GATHER_AXES = ((Y, X, Z), (X, Z, Y), (Z, Y, X), (Y, Z, X), (X, Y, Z), (Z, X, Y))
LIST_AXES = (Z, X, Y)
STAGE_AT = (0.0, 2.2, 5.6, 8.7, 12.7, 17.2, 22.7, 27.2)
CHOOSE_AT = 17.9


def plane_index(place, j):
    a, b = REDUCE_AXES[j]
    return place[a] * 4 + place[b]


def chip_index(place, axes):
    a, b, c = axes
    return place[c] * 16 + place[b] * 4 + place[a]


def gather_kernel(
    mom,
    vec,
    blk_in,
    own_in,
    picked,
    v,
    vt,
    vn,
    tw,
    tab,
    core_out,
    core_in,
    full,
    outbox,
    inbox,
    inbox2,
    every,
    lists,
    ids,
    chosen,
    rows,
    local_sem,
    core_sem,
    list_sem,
    rs_sem,
    ag_sem,
    last_sem,
    fwd_sem,
    sib_sem,
    row_sem,
):
    sites, width = v.shape[3], v.shape[4]
    colors = v.shape[2]
    rb = 2 * width // PLANE
    y = lax.axis_index("tm")
    sp = lax.axis_index("space")
    x, z, k = sp // 8, (sp // 2) % 4, sp % 2
    place = (y, x, z)

    def device(where, core):
        return (where[0], where[1] * 8 + where[2] * 2 + core)

    def ring(axis, offset):
        where = list(place)
        where[axis] = (place[axis] + offset) % RING
        return where[axis], device(where, k)

    sibling = device(place, 1 - k)

    def remote(src, dst, sems, to):
        return pltpu.make_async_remote_copy(
            src_ref=src, dst_ref=dst, send_sem=sems.at[0], recv_sem=sems.at[1], device_id=to, device_id_type=MESH
        )

    barrier = pltpu.get_barrier_semaphore()
    for axis in (Y, X, Z):
        for offset in (1, 2, 3):
            pl.semaphore_signal(barrier, inc=1, device_id=ring(axis, offset)[1], device_id_type=MESH)
    pl.semaphore_signal(barrier, inc=1, device_id=sibling, device_id_type=MESH)

    def load(n, c):
        slab = (1 - k) if n == 0 else k
        return pltpu.make_async_copy(vec.at[slab, :, c], v.at[n, :, c], local_sem.at[n * colors + c])

    for n in range(2):
        for c in range(colors):
            load(n, c).start()
    my_list = chip_index(place, LIST_AXES)
    load_blk = pltpu.make_async_copy(blk_in, lists.at[my_list, k, pl.ds(0, 1)], local_sem.at[2 * colors])
    load_own = pltpu.make_async_copy(own_in, lists.at[my_list, k, pl.ds(1, 1)], local_sem.at[2 * colors + 1])
    load_blk.start()
    load_own.start()

    def list_copies(stage):
        if stage == 0:
            ref = lists.at[my_list, k]
            return [remote(ref, ref, list_sem.at[:, 0, 0], sibling)]
        size = 4 ** (stage - 1)
        ref = lists.at[pl.ds(my_list // size * size, size)]
        axis = LIST_AXES[stage - 1]
        return [remote(ref, ref, list_sem.at[:, stage, o - 1], ring(axis, o)[1]) for o in (1, 2, 3)]

    def list_step(stage):
        if stage > 0:
            for copy in list_copies(stage - 1):
                copy.wait()
        if stage < 4:
            for copy in list_copies(stage):
                copy.start()

    lane = lax.broadcasted_iota(jnp.int32, (8, sites), 1)
    row = lax.broadcasted_iota(jnp.int32, (8, sites), 0)
    site = sp * sites + lane
    gx, gy, gz = site % LX, site // LX % LX, site // (LX * LX)

    def turns(p):
        return mom[p, 0] * gx + mom[p, 1] * gy + mom[p, 2] * gz

    turn = jnp.where(row < 2, turns(0), turns(1)) - (LX // 4) * (row % 2)
    tab[...] = jnp.transpose(jnp.cos((turn & (LX - 1)).astype(F32) * (2.0 * math.pi / LX)))

    def twist(n):
        for c in range(colors):
            load(n, c).wait()
            low, mid, high = 2 * c * sites, (2 * c + 1) * sites, (2 * c + 2) * sites
            vr, vi = v[n, 0, c], v[n, 1, c]
            tr, ti = jnp.transpose(vr), jnp.transpose(vi)
            vt[n, :, low:mid] = tr
            vt[n, :, mid:high] = ti
            vn[n, :, low:mid] = -ti
            vn[n, :, mid:high] = tr
            fr, fi = vr.astype(F32), vi.astype(F32)
            for p in range(2):
                cos = tab[:, 2 * p : 2 * p + 1]
                sin = tab[:, 2 * p + 1 : 2 * p + 2]
                real = (cos * fr + sin * fi).astype(BF)
                imag = (cos * fi - sin * fr).astype(BF)
                for jj in range(3):
                    cols = slice(jj * LANES, (jj + 1) * LANES)
                    tw[n, jj, low:mid, p * LANES : (p + 1) * LANES] = real[:, cols]
                    tw[n, jj, mid:high, p * LANES : (p + 1) * LANES] = imag[:, cols]

    def product(n, j):
        left = vn if j // 3 else vt
        return jnp.dot(left[n], tw[n, j % 3], preferred_element_type=F32)

    def pieces(j):
        for chip in range(PLANE):
            p, i = chip // (PLANE // 2), chip % (PLANE // 2)
            at = plane_index((0, chip // 4, chip % 4), j)
            yield at, slice(i * rb, (i + 1) * rb), slice(p * LANES, (p + 1) * LANES)

    def core_copy(h):
        return remote(core_out.at[h], core_in.at[h], core_sem.at[:, h], sibling)

    def rs1_copies(j):
        copies = []
        for o in (1, 2, 3):
            at, to = ring(REDUCE_AXES[j][0], o)
            copies.append(
                remote(outbox.at[j, pl.ds(at * 4, 4)], inbox.at[j, o - 1], rs_sem.at[:, j, 0, o - 1], to)
            )
        return copies

    def rs2_copies(j):
        copies = []
        for o in (1, 2, 3):
            at, to = ring(REDUCE_AXES[j][1], o)
            row_of = place[REDUCE_AXES[j][0]] * 4 + at
            copies.append(remote(outbox.at[j, row_of], inbox2.at[j, o - 1], rs_sem.at[:, j, 1, o - 1], to))
        return copies

    def rs1_start(j):
        for copy in rs1_copies(j):
            copy.start()

    def rs1_finish(j):
        for copy in rs1_copies(j):
            copy.wait_recv()
        base = place[REDUCE_AXES[j][0]] * 4
        for b in range(4):
            total = full[j, base + b]
            for o in range(3):
                total = total + inbox[j, o, b].astype(F32)
            full[j, base + b] = total
            outbox[j, base + b] = total.astype(BF)
        for copy in rs2_copies(j):
            copy.start()

    def rs2_finish(j):
        for copy in rs2_copies(j):
            copy.wait_recv()
        total = full[j, plane_index(place, j)]
        for o in range(3):
            total = total + inbox2[j, o].astype(F32)
        every[k, j, my_chip[j]] = total.astype(BF)

    my_chip = [chip_index(place, axes) for axes in GATHER_AXES]

    def block(j, start, size):
        return every.at[k, j, pl.ds(start, size)]

    def group(j, c, b):
        return block(j, c * 16 + b * 4, 4)

    def coords(j):
        a, b, c = GATHER_AXES[j]
        return place[a], place[b], place[c]

    def ag1_copies(j):
        ref = block(j, my_chip[j], 1)
        return [remote(ref, ref, ag_sem.at[:, j, 0, o - 1], ring(GATHER_AXES[j][0], o)[1]) for o in (1, 2, 3)]

    def ag2_copies(j):
        _, b, c = coords(j)
        ref = group(j, c, b)
        return [remote(ref, ref, ag_sem.at[:, j, 1, o - 1], ring(GATHER_AXES[j][1], o)[1]) for o in (1, 2, 3)]

    def ag3_copy(j, g, way):
        _, b, c = coords(j)
        ref = group(j, c, (b + g) % RING)
        return remote(ref, ref, last_sem.at[:, j, g, way], ring(GATHER_AXES[j][2], 1 if way == 0 else 3)[1])

    def fwd_copy(j, g):
        _, b, c = coords(j)
        way = g // 2
        source = (c + (3 if way == 0 else 1)) % RING
        ref = group(j, source, (b + g) % RING)
        return remote(ref, ref, fwd_sem.at[:, j, g], ring(GATHER_AXES[j][2], 1 if way == 0 else 3)[1])

    def sib_copy(j, n):
        _, b, c = coords(j)
        if n < 4:
            ref = group(j, c, (b + n) % RING)
        elif n < 6:
            ref = block(j, (c + (3 if n == 4 else 1)) % RING * 16, 16)
        else:
            ref = block(j, (c + 2) % RING * 16, 16)
        return remote(ref, ref, sib_sem.at[:, j, n], sibling)

    def ag1_start(j):
        for copy in ag1_copies(j):
            copy.start()

    def ag1_finish(j):
        for copy in ag1_copies(j):
            copy.wait_recv()
        for copy in ag2_copies(j):
            copy.start()
        for way in range(2):
            ag3_copy(j, 0, way).start()
        sib_copy(j, 0).start()

    def ag2_finish(j):
        for o, copy in zip((1, 2, 3), ag2_copies(j)):
            copy.wait_recv()
            g = 4 - o
            for way in range(2):
                ag3_copy(j, g, way).start()
            sib_copy(j, g).start()

    def ag3_finish(j):
        for g in range(4):
            ag3_copy(j, g, g // 2).wait_recv()
            fwd_copy(j, g).start()
        for g in range(4):
            ag3_copy(j, g, 1 - g // 2).wait_recv()
        sib_copy(j, 4).start()
        sib_copy(j, 5).start()

    def ag4_finish(j):
        for g in range(4):
            fwd_copy(j, g).wait_recv()
        sib_copy(j, 6).start()

    def make_table():
        me = y * 32 + sp
        at = lax.broadcasted_iota(jnp.int32, (CHIPS, LANES), 1)
        table = jnp.full((CHIPS, LANES), -1, jnp.int32)
        for core in range(2):
            listed = lists[:, core, 0, :] + 1
            hit = lists[:, core, 1, :] == me
            first = jnp.min(jnp.where(hit, at, LANES), axis=1, keepdims=True)
            last = jnp.max(jnp.where(hit, at, -1), axis=1, keepdims=True)
            one = jnp.sum(jnp.where(at == first, listed, 0), axis=1, keepdims=True) - 1
            two = jnp.sum(jnp.where((at == last) & (last > first), listed, 0), axis=1, keepdims=True) - 1
            table = jnp.where(at == 2 * core, one, jnp.where(at == 2 * core + 1, two, table))
        ids[...] = table


    own_rows = rb // 4
    out_rows = 4 * CAP * own_rows
    in_rows = 4 * rb
    rho = lax.broadcasted_iota(jnp.int32, (out_rows, CHIPS // 2), 0)
    kappa = lax.broadcasted_iota(jnp.int32, (out_rows, in_rows), 1).astype(F32)
    target = rho // (CAP * own_rows) * own_rows + rho // CAP % own_rows

    def choose_all():
        make_table()
        lane_ = lax.broadcasted_iota(jnp.int32, (out_rows, LANES), 1)
        row_ = lax.broadcasted_iota(jnp.int32, (out_rows, LANES), 0)
        which = row_ // (CAP * own_rows) * CAP + row_ % CAP
        want = target.astype(F32)
        for half in range(2):
            spread = jnp.where(which == half * 4 + lane_, jnp.where(lane_ < 4, rb, 0), 0).astype(F32).astype(BF)
            some = ids[pl.ds(half, CHIPS // 2, stride=2), :].astype(F32).astype(BF)
            want = want + lax.dot_general(spread, some, (((1,), (1,)), ((), ())), preferred_element_type=F32)
        for n in range(CHIPS // 2):
            chosen[n] = (kappa == want[:, n : n + 1]).astype(F32).astype(BF)

    def dots(j):
        total = product(0, j)
        for at, r, c in pieces(j):
            core_out[j, at] = total[r, c].astype(BF)
        total = product(1, j)
        for at, r, c in pieces(j):
            full[j, at] = total[r, c]
        if j == 0:
            pl.semaphore_wait(barrier, 10)
        core_copy(j).start()

    def core_finish(j):
        core_copy(j).wait_recv()
        total = full[j] + core_in[j].astype(F32)
        full[j] = total
        outbox[j] = total.astype(BF)
        rs1_start(j)

    def reduce_finish(j):
        rs2_finish(j)
        ag1_start(j)

    def first_list():
        load_blk.wait()
        load_own.wait()
        list_step(0)

    twist(0)
    twist(1)

    events = [(1.5, first_list, ())]
    events += [(t, list_step, (n + 1,)) for n, t in enumerate((3.7, 7.7, 11.6, 16.6))]
    events += [(CHOOSE_AT, choose_all, ())]
    for j in range(6):
        steps = (dots, core_finish, rs1_finish, reduce_finish, ag1_finish, ag2_finish, ag3_finish, ag4_finish)
        events += [(j + t, step, (j,)) for step, t in zip(steps, STAGE_AT)]
    for _, step, args in sorted(events, key=lambda e: e[0]):
        step(*args)
    for j in range(6):
        for n in range(7):
            sib_copy(j, n).wait_recv()

    def pick(n):
        gy_, g = n // 8, n % 8
        bands = []
        for u in range(2):
            for p in range(2):
                where = (gy_, p * 2 + g // 4, g % 4)
                bands.append(
                    jnp.concatenate([every[u, j, chip_index(where, GATHER_AXES[j])] for j in range(6)], axis=1)
                )
        return jnp.dot(chosen[n], jnp.concatenate(bands, axis=0), preferred_element_type=F32).astype(BF)

    chunk = 4 * out_rows

    def store(i):
        at = pl.ds(pl.multiple_of(i * chunk, chunk), chunk)
        return pltpu.make_async_copy(rows.at[at], picked.at[at], row_sem.at[i])

    def pick_four(i, carry):
        for n in range(4):
            at = pl.ds(pl.multiple_of((i * 4 + n) * out_rows, out_rows), out_rows)
            rows[at, :] = pick(i * 4 + n)
        store(i).start()
        return carry

    lax.fori_loop(0, 8, pick_four, 0)

    for j in range(6):
        core_copy(j).wait_send()
        for copy in rs1_copies(j) + rs2_copies(j) + ag1_copies(j) + ag2_copies(j):
            copy.wait_send()
        for g in range(4):
            for way in range(2):
                ag3_copy(j, g, way).wait_send()
            fwd_copy(j, g).wait_send()
        for n in range(7):
            sib_copy(j, n).wait_send()
    for i in range(8):
        store(i).wait()


def product_kernel(rows, pair, out, kernel):
    width = pair.shape[1]

    @pl.when(pl.program_id(0) == 0)
    def _():
        kernel[:width, :width] = pair[0]
        kernel[:width, width:] = pair[1]
        kernel[width:, :width] = -pair[1]
        kernel[width:, width:] = pair[0]

    y = jnp.dot(rows[...], kernel[...], preferred_element_type=F32).astype(BF)
    out[...] = y.reshape(out.shape)


def body(vectors, perambulators, item_block, item_owner, momenta):
    colors, sites, width = vectors.shape[2:]
    devices = 2 * CHIPS
    rb = 2 * width // PLANE
    own_rows = rb // 4
    total = devices * CAP * own_rows
    anywhere = pl.BlockSpec(memory_space=pl.ANY)
    picked = pl.pallas_call(
        gather_kernel,
        out_shape=jax.ShapeDtypeStruct((total, 2 * width), BF),
        in_specs=[pl.BlockSpec(memory_space=pltpu.SMEM), anywhere, anywhere, anywhere],
        out_specs=anywhere,
        scratch_shapes=[
            pltpu.VMEM((2, 2, colors, sites, width), BF),
            pltpu.VMEM((2, width, 2 * colors * sites), BF),
            pltpu.VMEM((2, width, 2 * colors * sites), BF),
            pltpu.VMEM((2, 3, 2 * colors * sites, 2 * LANES), BF),
            pltpu.VMEM((sites, 8), F32),
            pltpu.VMEM((6, PLANE, rb, LANES), BF),
            pltpu.VMEM((6, PLANE, rb, LANES), BF),
            pltpu.VMEM((6, PLANE, rb, LANES), F32),
            pltpu.VMEM((6, PLANE, rb, LANES), BF),
            pltpu.VMEM((6, 3, 4, rb, LANES), BF),
            pltpu.VMEM((6, 3, rb, LANES), BF),
            pltpu.VMEM((2, 6, CHIPS, rb, LANES), BF),
            pltpu.VMEM((CHIPS, 2, 2, LANES), jnp.int32),
            pltpu.VMEM((CHIPS, LANES), jnp.int32),
            pltpu.VMEM((CHIPS // 2, 8 * own_rows, 4 * rb), BF),
            pltpu.VMEM((total, 2 * width), BF),
            pltpu.SemaphoreType.DMA((2 * colors + 2,)),
            pltpu.SemaphoreType.DMA((2, 6)),
            pltpu.SemaphoreType.DMA((2, 4, 3)),
            pltpu.SemaphoreType.DMA((2, 6, 2, 3)),
            pltpu.SemaphoreType.DMA((2, 6, 2, 3)),
            pltpu.SemaphoreType.DMA((2, 6, 4, 2)),
            pltpu.SemaphoreType.DMA((2, 6, 4)),
            pltpu.SemaphoreType.DMA((2, 6, 7)),
            pltpu.SemaphoreType.DMA((8,)),
        ],
        compiler_params=pltpu.CompilerParams(
            collective_id=0, has_side_effects=True, vmem_limit_bytes=60 * 1024 * 1024
        ),
        name="gather_elementals",
    )(momenta, vectors, item_block, item_owner)
    tile = 384
    out = pl.pallas_call(
        product_kernel,
        out_shape=jax.ShapeDtypeStruct((total // 2, 2, 2 * width), BF),
        grid=(total // tile,),
        in_specs=[
            pl.BlockSpec((tile, 2 * width), lambda i: (i, 0)),
            pl.BlockSpec((2, width, width), lambda i: (0, 0, 0)),
        ],
        out_specs=pl.BlockSpec((tile // 2, 2, 2 * width), lambda i: (i, 0, 0)),
        scratch_shapes=[pltpu.VMEM((2 * width, 2 * width), BF)],
        compiler_params=pltpu.CompilerParams(vmem_limit_bytes=56 * 1024 * 1024),
        name="contract_perambulators",
    )(picked, perambulators[0])
    return out.reshape(1, devices, own_rows, CAP, 2 * width).transpose(0, 1, 3, 2, 4)


def solution(mesh):
    both = ("tm", "space")
    in_specs = (
        P("tm", None, None, "space", None),
        P(both, None, None, None),
        P(both, None),
        P(both, None),
        P(),
    )
    out_specs = P(both, None, None, None, None)
    return jax.shard_map(body, mesh=mesh, in_specs=in_specs, out_specs=out_specs, check_vma=False)
```

```python
import math

import jax
import jax.numpy as jnp
from jax import lax
from jax.experimental import pallas as pl
from jax.experimental.pallas import tpu as pltpu
from jax.sharding import PartitionSpec as P

LX = 64
CAP = 2
RING = 4
CHIPS = RING * RING * RING
PLANE = RING * RING
LANES = 128
BF = jnp.bfloat16
F32 = jnp.float32
MESH = pl.DeviceIdType.MESH

Y, X, Z = 0, 1, 2
REDUCE_AXES = ((X, Z), (Z, X), (X, Z), (Z, X), (X, Z), (Z, X))
GATHER_AXES = ((Y, X, Z), (X, Z, Y), (Z, Y, X), (Y, Z, X), (X, Y, Z), (Z, X, Y))
LIST_AXES = (Z, X, Y)
STAGE_AT = (0.0, 2.2, 5.6, 8.7, 12.7, 17.2, 22.7, 27.2)
CHOOSE_AT = 17.9


def plane_index(place, j):
    a, b = REDUCE_AXES[j]
    return place[a] * 4 + place[b]


def chip_index(place, axes):
    a, b, c = axes
    return place[c] * 16 + place[b] * 4 + place[a]


def gather_kernel(
    mom,
    vec,
    blk_in,
    own_in,
    picked,
    v,
    vt,
    vn,
    tw,
    tab,
    core_out,
    core_in,
    full,
    outbox,
    inbox,
    inbox2,
    every,
    lists,
    ids,
    chosen,
    rows,
    local_sem,
    core_sem,
    list_sem,
    rs_sem,
    ag_sem,
    last_sem,
    fwd_sem,
    sib_sem,
    row_sem,
):
    sites, width = v.shape[3], v.shape[4]
    colors = v.shape[2]
    rb = 2 * width // PLANE
    y = lax.axis_index("tm")
    sp = lax.axis_index("space")
    x, z, k = sp // 8, (sp // 2) % 4, sp % 2
    place = (y, x, z)

    def device(where, core):
        return (where[0], where[1] * 8 + where[2] * 2 + core)

    def ring(axis, offset):
        where = list(place)
        where[axis] = (place[axis] + offset) % RING
        return where[axis], device(where, k)

    sibling = device(place, 1 - k)

    def remote(src, dst, sems, to):
        return pltpu.make_async_remote_copy(
            src_ref=src, dst_ref=dst, send_sem=sems.at[0], recv_sem=sems.at[1], device_id=to, device_id_type=MESH
        )

    barrier = pltpu.get_barrier_semaphore()
    for axis in (Y, X, Z):
        for offset in (1, 2, 3):
            pl.semaphore_signal(barrier, inc=1, device_id=ring(axis, offset)[1], device_id_type=MESH)
    pl.semaphore_signal(barrier, inc=1, device_id=sibling, device_id_type=MESH)

    def load(n, c):
        slab = (1 - k) if n == 0 else k
        return pltpu.make_async_copy(vec.at[slab, :, c], v.at[n, :, c], local_sem.at[n * colors + c])

    for n in range(2):
        for c in range(colors):
            load(n, c).start()
    my_list = chip_index(place, LIST_AXES)
    load_blk = pltpu.make_async_copy(blk_in, lists.at[my_list, k, pl.ds(0, 1)], local_sem.at[2 * colors])
    load_own = pltpu.make_async_copy(own_in, lists.at[my_list, k, pl.ds(1, 1)], local_sem.at[2 * colors + 1])
    load_blk.start()
    load_own.start()

    def list_copies(stage):
        if stage == 0:
            ref = lists.at[my_list, k]
            return [remote(ref, ref, list_sem.at[:, 0, 0], sibling)]
        size = 4 ** (stage - 1)
        ref = lists.at[pl.ds(my_list // size * size, size)]
        axis = LIST_AXES[stage - 1]
        return [remote(ref, ref, list_sem.at[:, stage, o - 1], ring(axis, o)[1]) for o in (1, 2, 3)]

    def list_step(stage):
        if stage > 0:
            for copy in list_copies(stage - 1):
                copy.wait()
        if stage < 4:
            for copy in list_copies(stage):
                copy.start()

    lane = lax.broadcasted_iota(jnp.int32, (8, sites), 1)
    row = lax.broadcasted_iota(jnp.int32, (8, sites), 0)
    site = sp * sites + lane
    gx, gy, gz = site % LX, site // LX % LX, site // (LX * LX)

    def turns(p):
        return mom[p, 0] * gx + mom[p, 1] * gy + mom[p, 2] * gz

    turn = jnp.where(row < 2, turns(0), turns(1)) - (LX // 4) * (row % 2)
    tab[...] = jnp.transpose(jnp.cos((turn & (LX - 1)).astype(F32) * (2.0 * math.pi / LX)))

    def twist(n):
        for c in range(colors):
            load(n, c).wait()
            low, mid, high = 2 * c * sites, (2 * c + 1) * sites, (2 * c + 2) * sites
            vr, vi = v[n, 0, c], v[n, 1, c]
            tr, ti = jnp.transpose(vr), jnp.transpose(vi)
            vt[n, :, low:mid] = tr
            vt[n, :, mid:high] = ti
            vn[n, :, low:mid] = -ti
            vn[n, :, mid:high] = tr
            fr, fi = vr.astype(F32), vi.astype(F32)
            for p in range(2):
                cos = tab[:, 2 * p : 2 * p + 1]
                sin = tab[:, 2 * p + 1 : 2 * p + 2]
                real = (cos * fr + sin * fi).astype(BF)
                imag = (cos * fi - sin * fr).astype(BF)
                for jj in range(3):
                    cols = slice(jj * LANES, (jj + 1) * LANES)
                    tw[n, jj, low:mid, p * LANES : (p + 1) * LANES] = real[:, cols]
                    tw[n, jj, mid:high, p * LANES : (p + 1) * LANES] = imag[:, cols]

    def product(n, j):
        left = vn if j // 3 else vt
        return jnp.dot(left[n], tw[n, j % 3], preferred_element_type=F32)

    def pieces(j):
        for chip in range(PLANE):
            p, i = chip // (PLANE // 2), chip % (PLANE // 2)
            at = plane_index((0, chip // 4, chip % 4), j)
            yield at, slice(i * rb, (i + 1) * rb), slice(p * LANES, (p + 1) * LANES)

    def core_copy(h):
        return remote(core_out.at[h], core_in.at[h], core_sem.at[:, h], sibling)

    def rs1_copies(j):
        copies = []
        for o in (1, 2, 3):
            at, to = ring(REDUCE_AXES[j][0], o)
            copies.append(
                remote(outbox.at[j, pl.ds(at * 4, 4)], inbox.at[j, o - 1], rs_sem.at[:, j, 0, o - 1], to)
            )
        return copies

    def rs2_copies(j):
        copies = []
        for o in (1, 2, 3):
            at, to = ring(REDUCE_AXES[j][1], o)
            row_of = place[REDUCE_AXES[j][0]] * 4 + at
            copies.append(remote(outbox.at[j, row_of], inbox2.at[j, o - 1], rs_sem.at[:, j, 1, o - 1], to))
        return copies

    def rs1_start(j):
        for copy in rs1_copies(j):
            copy.start()

    def rs1_finish(j):
        for copy in rs1_copies(j):
            copy.wait_recv()
        base = place[REDUCE_AXES[j][0]] * 4
        for b in range(4):
            total = full[j, base + b]
            for o in range(3):
                total = total + inbox[j, o, b].astype(F32)
            full[j, base + b] = total
            outbox[j, base + b] = total.astype(BF)
        for copy in rs2_copies(j):
            copy.start()

    def rs2_finish(j):
        for copy in rs2_copies(j):
            copy.wait_recv()
        total = full[j, plane_index(place, j)]
        for o in range(3):
            total = total + inbox2[j, o].astype(F32)
        every[k, j, my_chip[j]] = total.astype(BF)

    my_chip = [chip_index(place, axes) for axes in GATHER_AXES]

    def block(j, start, size):
        return every.at[k, j, pl.ds(start, size)]

    def group(j, c, b):
        return block(j, c * 16 + b * 4, 4)

    def coords(j):
        a, b, c = GATHER_AXES[j]
        return place[a], place[b], place[c]

    def ag1_copies(j):
        ref = block(j, my_chip[j], 1)
        return [remote(ref, ref, ag_sem.at[:, j, 0, o - 1], ring(GATHER_AXES[j][0], o)[1]) for o in (1, 2, 3)]

    def ag2_copies(j):
        _, b, c = coords(j)
        ref = group(j, c, b)
        return [remote(ref, ref, ag_sem.at[:, j, 1, o - 1], ring(GATHER_AXES[j][1], o)[1]) for o in (1, 2, 3)]

    def ag3_copy(j, g, way):
        _, b, c = coords(j)
        ref = group(j, c, (b + g) % RING)
        return remote(ref, ref, last_sem.at[:, j, g, way], ring(GATHER_AXES[j][2], 1 if way == 0 else 3)[1])

    def fwd_copy(j, g):
        _, b, c = coords(j)
        way = g // 2
        source = (c + (3 if way == 0 else 1)) % RING
        ref = group(j, source, (b + g) % RING)
        return remote(ref, ref, fwd_sem.at[:, j, g], ring(GATHER_AXES[j][2], 1 if way == 0 else 3)[1])

    def sib_copy(j, n):
        _, b, c = coords(j)
        if n < 4:
            ref = group(j, c, (b + n) % RING)
        elif n < 6:
            ref = block(j, (c + (3 if n == 4 else 1)) % RING * 16, 16)
        else:
            ref = block(j, (c + 2) % RING * 16, 16)
        return remote(ref, ref, sib_sem.at[:, j, n], sibling)

    def ag1_start(j):
        for copy in ag1_copies(j):
            copy.start()

    def ag1_finish(j):
        for copy in ag1_copies(j):
            copy.wait_recv()
        for copy in ag2_copies(j):
            copy.start()
        for way in range(2):
            ag3_copy(j, 0, way).start()
        sib_copy(j, 0).start()

    def ag2_finish(j):
        for o, copy in zip((1, 2, 3), ag2_copies(j)):
            copy.wait_recv()
            g = 4 - o
            for way in range(2):
                ag3_copy(j, g, way).start()
            sib_copy(j, g).start()

    def ag3_finish(j):
        for g in range(4):
            ag3_copy(j, g, g // 2).wait_recv()
            fwd_copy(j, g).start()
        for g in range(4):
            ag3_copy(j, g, 1 - g // 2).wait_recv()
        sib_copy(j, 4).start()
        sib_copy(j, 5).start()

    def ag4_finish(j):
        for g in range(4):
            fwd_copy(j, g).wait_recv()
        sib_copy(j, 6).start()

    def make_table():
        me = y * 32 + sp
        at = lax.broadcasted_iota(jnp.int32, (CHIPS, LANES), 1)
        table = jnp.full((CHIPS, LANES), -1, jnp.int32)
        for core in range(2):
            listed = lists[:, core, 0, :] + 1
            hit = lists[:, core, 1, :] == me
            first = jnp.min(jnp.where(hit, at, LANES), axis=1, keepdims=True)
            last = jnp.max(jnp.where(hit, at, -1), axis=1, keepdims=True)
            one = jnp.sum(jnp.where(at == first, listed, 0), axis=1, keepdims=True) - 1
            two = jnp.sum(jnp.where((at == last) & (last > first), listed, 0), axis=1, keepdims=True) - 1
            table = jnp.where(at == 2 * core, one, jnp.where(at == 2 * core + 1, two, table))
        ids[...] = table


    own_rows = rb // 4
    out_rows = 4 * CAP * own_rows
    in_rows = 4 * rb
    rho = lax.broadcasted_iota(jnp.int32, (out_rows, CHIPS // 2), 0)
    kappa = lax.broadcasted_iota(jnp.int32, (out_rows, in_rows), 1).astype(F32)
    target = rho // (CAP * own_rows) * own_rows + rho // CAP % own_rows

    def choose_all():
        make_table()
        lane_ = lax.broadcasted_iota(jnp.int32, (out_rows, LANES), 1)
        row_ = lax.broadcasted_iota(jnp.int32, (out_rows, LANES), 0)
        which = row_ // (CAP * own_rows) * CAP + row_ % CAP
        want = target.astype(F32)
        for half in range(2):
            spread = jnp.where(which == half * 4 + lane_, jnp.where(lane_ < 4, rb, 0), 0).astype(F32).astype(BF)
            some = ids[pl.ds(half, CHIPS // 2, stride=2), :].astype(F32).astype(BF)
            want = want + lax.dot_general(spread, some, (((1,), (1,)), ((), ())), preferred_element_type=F32)
        for n in range(CHIPS // 2):
            chosen[n] = (kappa == want[:, n : n + 1]).astype(F32).astype(BF)

    def dots(j):
        total = product(0, j)
        for at, r, c in pieces(j):
            core_out[j, at] = total[r, c].astype(BF)
        total = product(1, j)
        for at, r, c in pieces(j):
            full[j, at] = total[r, c]
        if j == 0:
            pl.semaphore_wait(barrier, 10)
        core_copy(j).start()

    def core_finish(j):
        core_copy(j).wait_recv()
        total = full[j] + core_in[j].astype(F32)
        full[j] = total
        outbox[j] = total.astype(BF)
        rs1_start(j)

    def reduce_finish(j):
        rs2_finish(j)
        ag1_start(j)

    def first_list():
        load_blk.wait()
        load_own.wait()
        list_step(0)

    twist(0)
    twist(1)

    events = [(1.5, first_list, ())]
    events += [(t, list_step, (n + 1,)) for n, t in enumerate((3.7, 7.7, 11.6, 16.6))]
    events += [(CHOOSE_AT, choose_all, ())]
    for j in range(6):
        steps = (dots, core_finish, rs1_finish, reduce_finish, ag1_finish, ag2_finish, ag3_finish, ag4_finish)
        events += [(j + t, step, (j,)) for step, t in zip(steps, STAGE_AT)]
    for _, step, args in sorted(events, key=lambda e: e[0]):
        step(*args)
    for j in range(6):
        for n in range(7):
            sib_copy(j, n).wait_recv()

    def pick(n):
        gy_, g = n // 8, n % 8
        bands = []
        for u in range(2):
            for p in range(2):
                where = (gy_, p * 2 + g // 4, g % 4)
                bands.append(
                    jnp.concatenate([every[u, j, chip_index(where, GATHER_AXES[j])] for j in range(6)], axis=1)
                )
        return jnp.dot(chosen[n], jnp.concatenate(bands, axis=0), preferred_element_type=F32).astype(BF)

    chunk = 4 * out_rows

    def store(i):
        at = pl.ds(pl.multiple_of(i * chunk, chunk), chunk)
        return pltpu.make_async_copy(rows.at[at], picked.at[at], row_sem.at[i])

    def pick_four(i, carry):
        for n in range(4):
            at = pl.ds(pl.multiple_of((i * 4 + n) * out_rows, out_rows), out_rows)
            rows[at, :] = pick(i * 4 + n)
        store(i).start()
        return carry

    lax.fori_loop(0, 8, pick_four, 0)

    for j in range(6):
        core_copy(j).wait_send()
        for copy in rs1_copies(j) + rs2_copies(j) + ag1_copies(j) + ag2_copies(j):
            copy.wait_send()
        for g in range(4):
            for way in range(2):
                ag3_copy(j, g, way).wait_send()
            fwd_copy(j, g).wait_send()
        for n in range(7):
            sib_copy(j, n).wait_send()
    for i in range(8):
        store(i).wait()


def product_kernel(rows, pair, out, kernel):
    width = pair.shape[1]

    @pl.when(pl.program_id(0) == 0)
    def _():
        kernel[:width, :width] = pair[0]
        kernel[:width, width:] = pair[1]
        kernel[width:, :width] = -pair[1]
        kernel[width:, width:] = pair[0]

    y = jnp.dot(rows[...], kernel[...], preferred_element_type=F32).astype(BF)
    out[...] = y.reshape(out.shape)


def body(vectors, perambulators, item_block, item_owner, momenta):
    colors, sites, width = vectors.shape[2:]
    devices = 2 * CHIPS
    rb = 2 * width // PLANE
    own_rows = rb // 4
    total = devices * CAP * own_rows
    anywhere = pl.BlockSpec(memory_space=pl.ANY)
    picked = pl.pallas_call(
        gather_kernel,
        out_shape=jax.ShapeDtypeStruct((total, 2 * width), BF),
        in_specs=[pl.BlockSpec(memory_space=pltpu.SMEM), anywhere, anywhere, anywhere],
        out_specs=anywhere,
        scratch_shapes=[
            pltpu.VMEM((2, 2, colors, sites, width), BF),
            pltpu.VMEM((2, width, 2 * colors * sites), BF),
            pltpu.VMEM((2, width, 2 * colors * sites), BF),
            pltpu.VMEM((2, 3, 2 * colors * sites, 2 * LANES), BF),
            pltpu.VMEM((sites, 8), F32),
            pltpu.VMEM((6, PLANE, rb, LANES), BF),
            pltpu.VMEM((6, PLANE, rb, LANES), BF),
            pltpu.VMEM((6, PLANE, rb, LANES), F32),
            pltpu.VMEM((6, PLANE, rb, LANES), BF),
            pltpu.VMEM((6, 3, 4, rb, LANES), BF),
            pltpu.VMEM((6, 3, rb, LANES), BF),
            pltpu.VMEM((2, 6, CHIPS, rb, LANES), BF),
            pltpu.VMEM((CHIPS, 2, 2, LANES), jnp.int32),
            pltpu.VMEM((CHIPS, LANES), jnp.int32),
            pltpu.VMEM((CHIPS // 2, 8 * own_rows, 4 * rb), BF),
            pltpu.VMEM((total, 2 * width), BF),
            pltpu.SemaphoreType.DMA((2 * colors + 2,)),
            pltpu.SemaphoreType.DMA((2, 6)),
            pltpu.SemaphoreType.DMA((2, 4, 3)),
            pltpu.SemaphoreType.DMA((2, 6, 2, 3)),
            pltpu.SemaphoreType.DMA((2, 6, 2, 3)),
            pltpu.SemaphoreType.DMA((2, 6, 4, 2)),
            pltpu.SemaphoreType.DMA((2, 6, 4)),
            pltpu.SemaphoreType.DMA((2, 6, 7)),
            pltpu.SemaphoreType.DMA((8,)),
        ],
        compiler_params=pltpu.CompilerParams(
            collective_id=0, has_side_effects=True, vmem_limit_bytes=60 * 1024 * 1024
        ),
        name="gather_elementals",
    )(momenta, vectors, item_block, item_owner)
    tile = 768
    out = pl.pallas_call(
        product_kernel,
        out_shape=jax.ShapeDtypeStruct((total // 2, 2, 2 * width), BF),
        grid=(total // tile,),
        in_specs=[
            pl.BlockSpec((tile, 2 * width), lambda i: (i, 0)),
            pl.BlockSpec((2, width, width), lambda i: (0, 0, 0)),
        ],
        out_specs=pl.BlockSpec((tile // 2, 2, 2 * width), lambda i: (i, 0, 0)),
        scratch_shapes=[pltpu.VMEM((2 * width, 2 * width), BF)],
        compiler_params=pltpu.CompilerParams(vmem_limit_bytes=56 * 1024 * 1024),
        name="contract_perambulators",
    )(picked, perambulators[0])
    return out.reshape(1, devices, own_rows, CAP, 2 * width).transpose(0, 1, 3, 2, 4)


def solution(mesh):
    both = ("tm", "space")
    in_specs = (
        P("tm", None, None, "space", None),
        P(both, None, None, None),
        P(both, None),
        P(both, None),
        P(),
    )
    out_specs = P(both, None, None, None, None)
    return jax.shard_map(body, mesh=mesh, in_specs=in_specs, out_specs=out_specs, check_vma=False)
```

```python
import math

import jax
import jax.numpy as jnp
from jax import lax
from jax.experimental import pallas as pl
from jax.experimental.pallas import tpu as pltpu
from jax.sharding import PartitionSpec as P

LX = 64
CAP = 2
RING = 4
CHIPS = RING * RING * RING
PLANE = RING * RING
LANES = 128
BF = jnp.bfloat16
F32 = jnp.float32
MESH = pl.DeviceIdType.MESH

Y, X, Z = 0, 1, 2
REDUCE_AXES = ((X, Z), (Z, X), (X, Z), (Z, X), (X, Z), (Z, X))
GATHER_AXES = ((Y, X, Z), (X, Z, Y), (Z, Y, X), (Y, Z, X), (X, Y, Z), (Z, X, Y))
LIST_AXES = (Z, X, Y)
STAGE_AT = (0.0, 2.2, 5.6, 8.7, 12.7, 17.2, 22.7, 27.2)
CHOOSE_AT = 17.9


def plane_index(place, j):
    a, b = REDUCE_AXES[j]
    return place[a] * 4 + place[b]


def chip_index(place, axes):
    a, b, c = axes
    return place[c] * 16 + place[b] * 4 + place[a]


def gather_kernel(
    mom,
    vec,
    blk_in,
    own_in,
    picked,
    v,
    vt,
    vn,
    tw,
    tab,
    core_out,
    core_in,
    full,
    outbox,
    inbox,
    inbox2,
    every,
    lists,
    ids,
    chosen,
    rows,
    local_sem,
    core_sem,
    list_sem,
    rs_sem,
    ag_sem,
    last_sem,
    fwd_sem,
    sib_sem,
    row_sem,
):
    sites, width = v.shape[3], v.shape[4]
    colors = v.shape[2]
    rb = 2 * width // PLANE
    y = lax.axis_index("tm")
    sp = lax.axis_index("space")
    x, z, k = sp // 8, (sp // 2) % 4, sp % 2
    place = (y, x, z)

    def device(where, core):
        return (where[0], where[1] * 8 + where[2] * 2 + core)

    def ring(axis, offset):
        where = list(place)
        where[axis] = (place[axis] + offset) % RING
        return where[axis], device(where, k)

    sibling = device(place, 1 - k)

    def remote(src, dst, sems, to):
        return pltpu.make_async_remote_copy(
            src_ref=src, dst_ref=dst, send_sem=sems.at[0], recv_sem=sems.at[1], device_id=to, device_id_type=MESH
        )

    barrier = pltpu.get_barrier_semaphore()
    for axis in (Y, X, Z):
        for offset in (1, 2, 3):
            pl.semaphore_signal(barrier, inc=1, device_id=ring(axis, offset)[1], device_id_type=MESH)
    pl.semaphore_signal(barrier, inc=1, device_id=sibling, device_id_type=MESH)

    def load(n, c):
        slab = (1 - k) if n == 0 else k
        return pltpu.make_async_copy(vec.at[slab, :, c], v.at[n, :, c], local_sem.at[n * colors + c])

    for n in range(2):
        for c in range(colors):
            load(n, c).start()
    my_list = chip_index(place, LIST_AXES)
    load_blk = pltpu.make_async_copy(blk_in, lists.at[my_list, k, pl.ds(0, 1)], local_sem.at[2 * colors])
    load_own = pltpu.make_async_copy(own_in, lists.at[my_list, k, pl.ds(1, 1)], local_sem.at[2 * colors + 1])
    load_blk.start()
    load_own.start()

    def list_copies(stage):
        if stage == 0:
            ref = lists.at[my_list, k]
            return [remote(ref, ref, list_sem.at[:, 0, 0], sibling)]
        size = 4 ** (stage - 1)
        ref = lists.at[pl.ds(my_list // size * size, size)]
        axis = LIST_AXES[stage - 1]
        return [remote(ref, ref, list_sem.at[:, stage, o - 1], ring(axis, o)[1]) for o in (1, 2, 3)]

    def list_step(stage):
        if stage > 0:
            for copy in list_copies(stage - 1):
                copy.wait()
        if stage < 4:
            for copy in list_copies(stage):
                copy.start()

    lane = lax.broadcasted_iota(jnp.int32, (8, sites), 1)
    row = lax.broadcasted_iota(jnp.int32, (8, sites), 0)
    site = sp * sites + lane
    gx, gy, gz = site % LX, site // LX % LX, site // (LX * LX)

    def turns(p):
        return mom[p, 0] * gx + mom[p, 1] * gy + mom[p, 2] * gz

    turn = jnp.where(row < 2, turns(0), turns(1)) - (LX // 4) * (row % 2)
    tab[...] = jnp.transpose(jnp.cos((turn & (LX - 1)).astype(F32) * (2.0 * math.pi / LX)))

    def twist(n):
        for c in range(colors):
            load(n, c).wait()
            low, mid, high = 2 * c * sites, (2 * c + 1) * sites, (2 * c + 2) * sites
            vr, vi = v[n, 0, c], v[n, 1, c]
            tr, ti = jnp.transpose(vr), jnp.transpose(vi)
            vt[n, :, low:mid] = tr
            vt[n, :, mid:high] = ti
            vn[n, :, low:mid] = -ti
            vn[n, :, mid:high] = tr
            fr, fi = vr.astype(F32), vi.astype(F32)
            for p in range(2):
                cos = tab[:, 2 * p : 2 * p + 1]
                sin = tab[:, 2 * p + 1 : 2 * p + 2]
                real = (cos * fr + sin * fi).astype(BF)
                imag = (cos * fi - sin * fr).astype(BF)
                for jj in range(3):
                    cols = slice(jj * LANES, (jj + 1) * LANES)
                    tw[n, jj, low:mid, p * LANES : (p + 1) * LANES] = real[:, cols]
                    tw[n, jj, mid:high, p * LANES : (p + 1) * LANES] = imag[:, cols]

    def product(n, j):
        left = vn if j // 3 else vt
        return jnp.dot(left[n], tw[n, j % 3], preferred_element_type=F32)

    def pieces(j):
        for chip in range(PLANE):
            p, i = chip // (PLANE // 2), chip % (PLANE // 2)
            at = plane_index((0, chip // 4, chip % 4), j)
            yield at, slice(i * rb, (i + 1) * rb), slice(p * LANES, (p + 1) * LANES)

    def core_copy(h):
        return remote(core_out.at[h], core_in.at[h], core_sem.at[:, h], sibling)

    def rs1_copies(j):
        copies = []
        for o in (1, 2, 3):
            at, to = ring(REDUCE_AXES[j][0], o)
            copies.append(
                remote(outbox.at[j, pl.ds(at * 4, 4)], inbox.at[j, o - 1], rs_sem.at[:, j, 0, o - 1], to)
            )
        return copies

    def rs2_copies(j):
        copies = []
        for o in (1, 2, 3):
            at, to = ring(REDUCE_AXES[j][1], o)
            row_of = place[REDUCE_AXES[j][0]] * 4 + at
            copies.append(remote(outbox.at[j, row_of], inbox2.at[j, o - 1], rs_sem.at[:, j, 1, o - 1], to))
        return copies

    def rs1_start(j):
        for copy in rs1_copies(j):
            copy.start()

    def rs1_finish(j):
        for copy in rs1_copies(j):
            copy.wait_recv()
        base = place[REDUCE_AXES[j][0]] * 4
        for b in range(4):
            total = full[j, base + b]
            for o in range(3):
                total = total + inbox[j, o, b].astype(F32)
            full[j, base + b] = total
            outbox[j, base + b] = total.astype(BF)
        for copy in rs2_copies(j):
            copy.start()

    def rs2_finish(j):
        for copy in rs2_copies(j):
            copy.wait_recv()
        total = full[j, plane_index(place, j)]
        for o in range(3):
            total = total + inbox2[j, o].astype(F32)
        every[k, j, my_chip[j]] = total.astype(BF)

    my_chip = [chip_index(place, axes) for axes in GATHER_AXES]

    def block(j, start, size):
        return every.at[k, j, pl.ds(start, size)]

    def group(j, c, b):
        return block(j, c * 16 + b * 4, 4)

    def coords(j):
        a, b, c = GATHER_AXES[j]
        return place[a], place[b], place[c]

    def ag1_copies(j):
        ref = block(j, my_chip[j], 1)
        return [remote(ref, ref, ag_sem.at[:, j, 0, o - 1], ring(GATHER_AXES[j][0], o)[1]) for o in (1, 2, 3)]

    def ag2_copies(j):
        _, b, c = coords(j)
        ref = group(j, c, b)
        return [remote(ref, ref, ag_sem.at[:, j, 1, o - 1], ring(GATHER_AXES[j][1], o)[1]) for o in (1, 2, 3)]

    def ag3_copy(j, g, way):
        _, b, c = coords(j)
        ref = group(j, c, (b + g) % RING)
        return remote(ref, ref, last_sem.at[:, j, g, way], ring(GATHER_AXES[j][2], 1 if way == 0 else 3)[1])

    def fwd_copy(j, g):
        _, b, c = coords(j)
        way = g // 2
        source = (c + (3 if way == 0 else 1)) % RING
        ref = group(j, source, (b + g) % RING)
        return remote(ref, ref, fwd_sem.at[:, j, g], ring(GATHER_AXES[j][2], 1 if way == 0 else 3)[1])

    def sib_copy(j, n):
        _, b, c = coords(j)
        if n < 4:
            ref = group(j, c, (b + n) % RING)
        elif n < 6:
            ref = block(j, (c + (3 if n == 4 else 1)) % RING * 16, 16)
        else:
            ref = block(j, (c + 2) % RING * 16, 16)
        return remote(ref, ref, sib_sem.at[:, j, n], sibling)

    def ag1_start(j):
        for copy in ag1_copies(j):
            copy.start()

    def ag1_finish(j):
        for copy in ag1_copies(j):
            copy.wait_recv()
        for copy in ag2_copies(j):
            copy.start()
        for way in range(2):
            ag3_copy(j, 0, way).start()
        sib_copy(j, 0).start()

    def ag2_finish(j):
        for o, copy in zip((1, 2, 3), ag2_copies(j)):
            copy.wait_recv()
            g = 4 - o
            for way in range(2):
                ag3_copy(j, g, way).start()
            sib_copy(j, g).start()

    def ag3_finish(j):
        for g in range(4):
            ag3_copy(j, g, g // 2).wait_recv()
            fwd_copy(j, g).start()
        for g in range(4):
            ag3_copy(j, g, 1 - g // 2).wait_recv()
        sib_copy(j, 4).start()
        sib_copy(j, 5).start()

    def ag4_finish(j):
        for g in range(4):
            fwd_copy(j, g).wait_recv()
        sib_copy(j, 6).start()

    def make_table():
        me = y * 32 + sp
        at = lax.broadcasted_iota(jnp.int32, (CHIPS, LANES), 1)
        table = jnp.full((CHIPS, LANES), -1, jnp.int32)
        for core in range(2):
            listed = lists[:, core, 0, :] + 1
            hit = lists[:, core, 1, :] == me
            first = jnp.min(jnp.where(hit, at, LANES), axis=1, keepdims=True)
            last = jnp.max(jnp.where(hit, at, -1), axis=1, keepdims=True)
            one = jnp.sum(jnp.where(at == first, listed, 0), axis=1, keepdims=True) - 1
            two = jnp.sum(jnp.where((at == last) & (last > first), listed, 0), axis=1, keepdims=True) - 1
            table = jnp.where(at == 2 * core, one, jnp.where(at == 2 * core + 1, two, table))
        ids[...] = table


    own_rows = rb // 4
    out_rows = 4 * CAP * own_rows
    in_rows = 4 * rb
    rho = lax.broadcasted_iota(jnp.int32, (out_rows, CHIPS // 2), 0)
    kappa = lax.broadcasted_iota(jnp.int32, (out_rows, in_rows), 1).astype(F32)
    target = rho // (CAP * own_rows) * own_rows + rho // CAP % own_rows

    def choose_all():
        make_table()
        lane_ = lax.broadcasted_iota(jnp.int32, (out_rows, LANES), 1)
        row_ = lax.broadcasted_iota(jnp.int32, (out_rows, LANES), 0)
        which = row_ // (CAP * own_rows) * CAP + row_ % CAP
        want = target.astype(F32)
        for half in range(2):
            spread = jnp.where(which == half * 4 + lane_, jnp.where(lane_ < 4, rb, 0), 0).astype(F32).astype(BF)
            some = ids[pl.ds(half, CHIPS // 2, stride=2), :].astype(F32).astype(BF)
            want = want + lax.dot_general(spread, some, (((1,), (1,)), ((), ())), preferred_element_type=F32)
        for n in range(CHIPS // 2):
            chosen[n] = (kappa == want[:, n : n + 1]).astype(F32).astype(BF)

    def dots(j):
        total = product(0, j)
        for at, r, c in pieces(j):
            core_out[j, at] = total[r, c].astype(BF)
        total = product(1, j)
        for at, r, c in pieces(j):
            full[j, at] = total[r, c]
        if j == 0:
            pl.semaphore_wait(barrier, 10)
        core_copy(j).start()

    def core_finish(j):
        core_copy(j).wait_recv()
        total = full[j] + core_in[j].astype(F32)
        full[j] = total
        outbox[j] = total.astype(BF)
        rs1_start(j)

    def reduce_finish(j):
        rs2_finish(j)
        ag1_start(j)

    def first_list():
        load_blk.wait()
        load_own.wait()
        list_step(0)

    twist(0)
    twist(1)

    events = [(1.5, first_list, ())]
    events += [(t, list_step, (n + 1,)) for n, t in enumerate((3.7, 7.7, 11.6, 16.6))]
    events += [(CHOOSE_AT, choose_all, ())]
    for j in range(6):
        steps = (dots, core_finish, rs1_finish, reduce_finish, ag1_finish, ag2_finish, ag3_finish, ag4_finish)
        events += [(j + t, step, (j,)) for step, t in zip(steps, STAGE_AT)]
    for _, step, args in sorted(events, key=lambda e: e[0]):
        step(*args)
    for j in range(6):
        for n in range(7):
            sib_copy(j, n).wait_recv()

    def pick(n):
        gy_, g = n // 8, n % 8
        bands = []
        for u in range(2):
            for p in range(2):
                where = (gy_, p * 2 + g // 4, g % 4)
                bands.append(
                    jnp.concatenate([every[u, j, chip_index(where, GATHER_AXES[j])] for j in range(6)], axis=1)
                )
        return jnp.dot(chosen[n], jnp.concatenate(bands, axis=0), preferred_element_type=F32).astype(BF)

    chunk = 8 * out_rows

    def store(i):
        at = pl.ds(pl.multiple_of(i * chunk, chunk), chunk)
        return pltpu.make_async_copy(rows.at[at], picked.at[at], row_sem.at[i])

    def pick_eight(i, carry):
        for n in range(8):
            at = pl.ds(pl.multiple_of((i * 8 + n) * out_rows, out_rows), out_rows)
            rows[at, :] = pick(i * 8 + n)
        store(i).start()
        return carry

    lax.fori_loop(0, 4, pick_eight, 0)

    for j in range(6):
        core_copy(j).wait_send()
        for copy in rs1_copies(j) + rs2_copies(j) + ag1_copies(j) + ag2_copies(j):
            copy.wait_send()
        for g in range(4):
            for way in range(2):
                ag3_copy(j, g, way).wait_send()
            fwd_copy(j, g).wait_send()
        for n in range(7):
            sib_copy(j, n).wait_send()
    for i in range(4):
        store(i).wait()


def product_kernel(rows, pair, out, kernel):
    width = pair.shape[1]

    @pl.when(pl.program_id(0) == 0)
    def _():
        kernel[:width, :width] = pair[0]
        kernel[:width, width:] = pair[1]
        kernel[width:, :width] = -pair[1]
        kernel[width:, width:] = pair[0]

    y = jnp.dot(rows[...], kernel[...], preferred_element_type=F32).astype(BF)
    out[...] = y.reshape(out.shape)


def body(vectors, perambulators, item_block, item_owner, momenta):
    colors, sites, width = vectors.shape[2:]
    devices = 2 * CHIPS
    rb = 2 * width // PLANE
    own_rows = rb // 4
    total = devices * CAP * own_rows
    anywhere = pl.BlockSpec(memory_space=pl.ANY)
    picked = pl.pallas_call(
        gather_kernel,
        out_shape=jax.ShapeDtypeStruct((total, 2 * width), BF),
        in_specs=[pl.BlockSpec(memory_space=pltpu.SMEM), anywhere, anywhere, anywhere],
        out_specs=anywhere,
        scratch_shapes=[
            pltpu.VMEM((2, 2, colors, sites, width), BF),
            pltpu.VMEM((2, width, 2 * colors * sites), BF),
            pltpu.VMEM((2, width, 2 * colors * sites), BF),
            pltpu.VMEM((2, 3, 2 * colors * sites, 2 * LANES), BF),
            pltpu.VMEM((sites, 8), F32),
            pltpu.VMEM((6, PLANE, rb, LANES), BF),
            pltpu.VMEM((6, PLANE, rb, LANES), BF),
            pltpu.VMEM((6, PLANE, rb, LANES), F32),
            pltpu.VMEM((6, PLANE, rb, LANES), BF),
            pltpu.VMEM((6, 3, 4, rb, LANES), BF),
            pltpu.VMEM((6, 3, rb, LANES), BF),
            pltpu.VMEM((2, 6, CHIPS, rb, LANES), BF),
            pltpu.VMEM((CHIPS, 2, 2, LANES), jnp.int32),
            pltpu.VMEM((CHIPS, LANES), jnp.int32),
            pltpu.VMEM((CHIPS // 2, 8 * own_rows, 4 * rb), BF),
            pltpu.VMEM((total, 2 * width), BF),
            pltpu.SemaphoreType.DMA((2 * colors + 2,)),
            pltpu.SemaphoreType.DMA((2, 6)),
            pltpu.SemaphoreType.DMA((2, 4, 3)),
            pltpu.SemaphoreType.DMA((2, 6, 2, 3)),
            pltpu.SemaphoreType.DMA((2, 6, 2, 3)),
            pltpu.SemaphoreType.DMA((2, 6, 4, 2)),
            pltpu.SemaphoreType.DMA((2, 6, 4)),
            pltpu.SemaphoreType.DMA((2, 6, 7)),
            pltpu.SemaphoreType.DMA((4,)),
        ],
        compiler_params=pltpu.CompilerParams(
            collective_id=0, has_side_effects=True, vmem_limit_bytes=60 * 1024 * 1024
        ),
        name="gather_elementals",
    )(momenta, vectors, item_block, item_owner)
    tile = 768
    out = pl.pallas_call(
        product_kernel,
        out_shape=jax.ShapeDtypeStruct((total // 2, 2, 2 * width), BF),
        grid=(total // tile,),
        in_specs=[
            pl.BlockSpec((tile, 2 * width), lambda i: (i, 0)),
            pl.BlockSpec((2, width, width), lambda i: (0, 0, 0)),
        ],
        out_specs=pl.BlockSpec((tile // 2, 2, 2 * width), lambda i: (i, 0, 0)),
        scratch_shapes=[pltpu.VMEM((2 * width, 2 * width), BF)],
        compiler_params=pltpu.CompilerParams(vmem_limit_bytes=56 * 1024 * 1024),
        name="contract_perambulators",
    )(picked, perambulators[0])
    return out.reshape(1, devices, own_rows, CAP, 2 * width).transpose(0, 1, 3, 2, 4)


def solution(mesh):
    both = ("tm", "space")
    in_specs = (
        P("tm", None, None, "space", None),
        P(both, None, None, None),
        P(both, None),
        P(both, None),
        P(),
    )
    out_specs = P(both, None, None, None, None)
    return jax.shard_map(body, mesh=mesh, in_specs=in_specs, out_specs=out_specs, check_vma=False)
```
